256 devices in a mesh: section: 8 (over x, z_lo), mp: 32 (over y, z_hi, core).
Axes of the slice: x: 4, y: 4, z: 8 (z_hi: 4, z_lo: 2; z = z_hi * 2 + z_lo), core: 2. Of those that a mesh axis runs over, the one named last changes fastest.
Arguments:
- enc_final: bfloat16 [8, 128, 4096], P('section', None, 'mp'), may hold values from -64 to 64
- enc_len: int32 [8], replicated, may hold values from 32 to 128, as said below
- kv_weight: bfloat16 [8, 4096, 2, 4096], P('section', None, None, 'mp'), may hold values from -1 to 1
- queries: bfloat16 [8, 8, 512, 4096], P('section', None, None, 'mp'), may hold values from -4096 to 4096
- d_context: bfloat16 [8, 8, 512, 4096], P('section', None, None, 'mp'), may hold values from -6 to 6
Outputs:
- context: bfloat16 [8, 8, 512, 4096], P('section', None, None, 'mp')
- query_grad: bfloat16 [8, 8, 512, 4096], P('section', None, None, 'mp')
- kv_weight_grad: bfloat16 [8, 4096, 2, 4096], P('section', None, None, 'mp')
- enc_grad: bfloat16 [8, 128, 4096], P('section', None, 'mp')
The draws below stay inside these ranges and needn't reach their ends.
Inputs may be any that keep to these rules, and one draw needn't show every extreme that they name: `enc_len`: some microbatch has exactly 128 valid positions.
All inputs are finite; a program needn't handle non-finite values.
Results may differ from the reference program's by a relative error of at most 0.02.
Values may be sent and summed in bfloat16 or wider, within the bound.
No kernel may reach another device: no remote copies, remote signals or barrier semaphores. Data moves between devices by JAX's collectives and lax.ppermute only.
A program may use at most 128 MiB of HBM per device.

```python
import jax
import jax.numpy as jnp
from jax import lax

D = 4096
HEADS = 64
HD = 64
SRC = 128
TGT = 512
MICRO = 8
N_SECTION = 8


def encoder_draw(key):
    drawn = jnp.clip(jax.random.normal(jax.random.fold_in(key, 101), (MICRO, SRC, D), jnp.float32), -6.0, 6.0)
    return drawn


def weight_draw(key):
    drawn = jnp.clip(jax.random.normal(jax.random.fold_in(key, 201), (N_SECTION, D, 2, D), jnp.float32), -6.0, 6.0)
    return drawn * D ** (-0.5)


def draw_enc_final(key, part):
    return encoder_draw(key).astype(jnp.bfloat16)


def draw_kv_weight(key, part):
    return weight_draw(key).astype(jnp.bfloat16)


def draw_enc_len(key, part):
    quarter = SRC // 4
    lengths = jax.random.randint(jax.random.fold_in(key, 601), (MICRO,), quarter, SRC)
    chosen = jax.random.randint(jax.random.fold_in(key, 602), (), 0, MICRO)
    lengths = lengths.at[chosen].set(SRC)
    return lengths.astype(jnp.int32)


def draw_queries(key, part):
    drawn = jnp.clip(jax.random.normal(jax.random.fold_in(key, 301), (N_SECTION, MICRO, TGT, D), jnp.float32), -6.0, 6.0)
    return drawn.astype(jnp.bfloat16)


def block_levels(key, dims, cuts, low, largest):
    def one(axis_at, parts):
        heights = jax.random.uniform(jax.random.fold_in(jax.random.fold_in(key, 6), axis_at), (parts,), jnp.float32, low / len(cuts), largest / len(cuts))
        return jnp.repeat(jnp.exp(heights), dims[axis_at] // parts).reshape((-1,) + (1,) * (len(dims) - axis_at - 1))

    loudness = one(*cuts[0])
    for cut in cuts[1:]:
        loudness = loudness * one(*cut)
    return loudness


def bell_draw(own_key, extent, scale, most, pieces=(), kind=jnp.bfloat16):
    gain = block_levels(own_key, extent, pieces, -0.22, 0.18) if pieces else 1.0
    array = jax.random.normal(own_key, extent, jnp.float32) * scale * gain
    return jnp.minimum(jnp.maximum(array, -most), most).astype(kind)


def setup_inputs(seed: int = 0) -> dict:
    key_of = jax.random.split(jax.random.key(seed), 6)
    enc_final = draw_enc_final(jax.random.fold_in(key_of[5], 71), 0)
    enc_len = draw_enc_len(jax.random.fold_in(key_of[5], 71), 0)
    kv_weight = draw_kv_weight(jax.random.fold_in(key_of[5], 71), 0)
    queries = draw_queries(jax.random.fold_in(key_of[5], 71), 0)
    d_context = bell_draw(key_of[4], (N_SECTION, MICRO, TGT, D), 1.0, 6.0, ((0, 8), (3, 32)))
    return {"enc_final": enc_final, "enc_len": enc_len, "kv_weight": kv_weight, "queries": queries, "d_context": d_context}


def layer_terms(enc_flat, valid_key, weight, query_in, grad_in):
    weight_flat = weight.reshape(D, 2 * D)
    key_value = jnp.dot(enc_flat, weight_flat, preferred_element_type=jnp.float32).astype(jnp.bfloat16)
    key_value = lax.optimization_barrier(key_value).astype(jnp.float32).reshape(MICRO, SRC, 2, HEADS, HD)
    key_heads = key_value[:, :, 0]
    value_heads = key_value[:, :, 1]
    query_heads = query_in.reshape(MICRO, TGT, HEADS, HD).astype(jnp.float32)
    grad_heads = grad_in.reshape(MICRO, TGT, HEADS, HD).astype(jnp.float32)
    factor = HD ** -0.5
    scores = jnp.einsum('mthd,mshd->mhts', query_heads, key_heads) * factor
    scores = jnp.where(valid_key[:, None, None, :], scores, -1e30)
    row_peak = jnp.max(scores, axis=-1, keepdims=True)
    exponent = jnp.exp(scores - row_peak)
    attn_prob = exponent / jnp.sum(exponent, axis=-1, keepdims=True)
    rounded = lax.optimization_barrier(attn_prob.astype(jnp.bfloat16)).astype(jnp.float32)
    context = jnp.einsum('mhts,mshd->mthd', rounded, value_heads).astype(jnp.bfloat16)
    value_grad = jnp.einsum('mhts,mthd->mshd', rounded, grad_heads)
    prob_grad = jnp.einsum('mthd,mshd->mhts', grad_heads, value_heads)
    score_grad = attn_prob * (prob_grad - jnp.sum(prob_grad * attn_prob, axis=-1, keepdims=True))
    score_rounded = lax.optimization_barrier((score_grad * factor).astype(jnp.bfloat16)).astype(jnp.float32)
    key_grad = jnp.einsum('mhts,mthd->mshd', score_rounded, query_heads)
    query_grad = jnp.einsum('mhts,mshd->mthd', score_rounded, key_heads).astype(jnp.bfloat16)
    kv_grad = jnp.stack([key_grad, value_grad], axis=2).astype(jnp.bfloat16).reshape(MICRO * SRC, 2 * D)
    weight_grad = lax.dot_general(enc_flat, kv_grad, (((0,), (0,)), ((), ())), preferred_element_type=jnp.float32).astype(jnp.bfloat16)
    enc_term = lax.dot_general(kv_grad, weight_flat, (((1,), (1,)), ((), ())), preferred_element_type=jnp.float32)
    return context.reshape(MICRO, TGT, D), query_grad.reshape(MICRO, TGT, D), weight_grad.reshape(D, 2, D), enc_term


def reference(enc_final, enc_len, kv_weight, queries, d_context):
    enc_flat = enc_final.reshape(MICRO * SRC, D)
    valid_key = jnp.arange(SRC, dtype=jnp.int32)[None, :] < enc_len[:, None]

    def advance(running, layer_in):
        weight, query_in, grad_in = layer_in
        context, query_grad, weight_grad, enc_term = layer_terms(enc_flat, valid_key, weight, query_in, grad_in)
        return running + enc_term, (context, query_grad, weight_grad)

    running, stacked = lax.scan(advance, jnp.zeros((MICRO * SRC, D), jnp.float32), (kv_weight, queries, d_context))
    context, query_grad, weight_grad = stacked
    return context, query_grad, weight_grad, running.reshape(MICRO, SRC, D).astype(jnp.bfloat16)
```

```python
import functools

import jax
import jax.numpy as jnp
from jax import lax
from jax.experimental import pallas as pl
from jax.experimental.pallas import tpu as pltpu
from jax.sharding import PartitionSpec as P

HD = 64
AXES = ("section", "mp")
BF = jnp.bfloat16
F32 = jnp.float32


def coords(i):
    section, mp = divmod(i, 32)
    x, zl = divmod(section, 2)
    y, zh, c = mp // 8, (mp // 2) % 4, mp % 2
    return x, y, 2 * zh + zl, c


def index(x, y, z, c):
    return ((x % 4) * 2 + z % 2) * 32 + (y % 4) * 8 + ((z % 8) // 2) * 2 + c


def shift(value, dx=0, dy=0, dz=0, dc=0):
    pairs = []
    for i in range(256):
        x, y, z, c = coords(i)
        pairs.append((i, index(x + dx, y + dy, z + dz, c ^ dc)))
    return lax.ppermute(value, AXES, pairs)


def nt(a, b):
    return lax.dot_general(a, b, (((1,), (1,)), ((), ())), preferred_element_type=F32)


def nn(a, b):
    return lax.dot_general(a, b, (((1,), (0,)), ((), ())), preferred_element_type=F32)


def tn(a, b):
    return lax.dot_general(a, b, (((0,), (0,)), ((), ())), preferred_element_type=F32)


def states_block(a, b, dy, zh, z):
    rows = []
    for dx in range(4):
        for zl in range(2):
            dz = (z + 8 - (2 * zh + zl)) & 7
            rows.append(a[dy][dx, dz])
            rows.append(b[dx][dy, dz])
    return jnp.concatenate(rows, axis=0)


def project_kernel(pos, *refs):
    a, b = refs[0:4], refs[4:8]
    w_own, w_par, keep, send, acc_own, acc_par = refs[8:]
    x, y, z = pos[0], pos[1], pos[2]
    for dy in range(4):
        for zh in range(4):
            lhs = states_block(a, b, dy, zh, z)
            f = ((y + 4 - dy) & 3) * 4 + zh
            own = nn(lhs, w_own[f])
            par = nn(lhs, w_par[f])
            if dy == 0 and zh == 0:
                acc_own[...] = own
                acc_par[...] = par
            else:
                acc_own[...] += own
                acc_par[...] += par
    for dx in range(4):
        for zl in range(2):
            m = ((x + 4 - dx) & 3) * 2 + zl
            row = (dx * 2 + zl) * 64
            keep[m] = acc_own[row : row + 64].astype(BF)
            send[m] = acc_par[row : row + 64].astype(BF)


def attend_kernel(pos, lens, q_ref, d_ref, keep_ref, recv_ref, ctx_ref, qg_ref, own_ref, part_ref):
    c = pos[3]
    q = q_ref[0, 0]
    d = d_ref[0, 0]
    kv = jnp.concatenate([keep_ref[0], recv_ref[0]], axis=0)
    k, v = kv[:, :128], kv[:, 128:]
    left = lax.broadcasted_iota(jnp.int32, (128, 128), 1) < HD
    top = lax.broadcasted_iota(jnp.int32, (128, 128), 0) < HD
    zero = jnp.zeros((128, 128), BF)

    def stack_heads(t):
        return jnp.concatenate([jnp.where(left, t, zero), jnp.where(left, zero, t)], axis=0)

    def stack_heads_t(t):
        tt = t.T
        return jnp.concatenate([jnp.where(top, tt, zero), jnp.where(top, zero, tt)], axis=1)

    k_rows, v_rows = stack_heads(k), stack_heads(v)
    k_cols, v_cols = stack_heads_t(k), stack_heads_t(v)
    factor = HD ** (-0.5)
    source = (lax.broadcasted_iota(jnp.int32, (128, 512), 0) + 64 * c) & 127
    valid = source < lens[pl.program_id(0)]
    scores = nt(k_rows, q)
    prob_grad = nt(v_rows, d)
    probs, score_grads = [], []
    for h in range(2):
        s = jnp.where(valid, scores[h * 128 : h * 128 + 128] * factor, -1e30)
        e = jnp.exp(s - jnp.max(s, axis=0, keepdims=True))
        p = e * (1.0 / jnp.sum(e, axis=0, keepdims=True))
        g = prob_grad[h * 128 : h * 128 + 128]
        score_grads.append((p * (g - jnp.sum(g * p, axis=0, keepdims=True)) * factor).astype(BF))
        probs.append(p.astype(BF))
    prob = jnp.concatenate(probs, axis=0)
    score_grad = jnp.concatenate(score_grads, axis=0)
    ctx_ref[0, 0] = nn(v_cols, prob).T.astype(BF)
    qg_ref[0, 0] = nn(k_cols, score_grad).T.astype(BF)
    vg = nn(prob, d)
    kg = nn(score_grad, q)
    kg = jnp.where(left, kg[:128], kg[128:]).astype(BF)
    vg = jnp.where(left, vg[:128], vg[128:]).astype(BF)
    own_ref[0, :, :128] = kg[:64]
    own_ref[0, :, 128:] = vg[:64]
    part_ref[0, :, :128] = kg[64:]
    part_ref[0, :, 128:] = vg[64:]


def spread_kernel(pos, g_own, g_par, w_own, w_par, *refs):
    a, b = refs[0:4], refs[4:8]
    x, y, z = pos[0], pos[1], pos[2]
    order = [(dx, zl, ((x + dx) & 3) * 2 + zl) for dx in range(4) for zl in range(2)]
    own = jnp.concatenate([g_own[m] for _, _, m in order], axis=0)
    par = jnp.concatenate([g_par[m] for _, _, m in order], axis=0)
    for dy in range(4):
        for zh in range(4):
            f = ((y + dy) & 3) * 4 + zh
            t = (nt(own, w_own[f]) + nt(par, w_par[f])).astype(BF)
            for dx, zl, _ in order:
                dz = (2 * zh + zl + 8 - z) & 7
                row = (dx * 2 + zl) * 64
                a[dy][dx, dz] = t[row : row + 32]
                b[dx][dy, dz] = t[row + 32 : row + 64]


def weight_kernel(pos, *refs):
    a, b = refs[0:4], refs[4:8]
    g_own, g_par, own_ref, par_ref = refs[8:]
    x, y, z = pos[0], pos[1], pos[2]
    order = [((x + 4 - dx) & 3) * 2 + zl for dx in range(4) for zl in range(2)]
    own = jnp.concatenate([g_own[m] for m in order], axis=0)
    par = jnp.concatenate([g_par[m] for m in order], axis=0)
    for dy in range(4):
        for zh in range(4):
            lhs = states_block(a, b, dy, zh, z)
            f = ((y + 4 - dy) & 3) * 4 + zh
            own_ref[f] = tn(lhs, own)
            par_ref[f] = tn(lhs, par).astype(BF)


SMEM = pl.BlockSpec(memory_space=pltpu.SMEM)
VMEM = pl.BlockSpec(memory_space=pltpu.VMEM)


def whole(kernel, n_in, outs, scratch=(), name=None):
    return pl.pallas_call(
        kernel,
        in_specs=[SMEM] + [VMEM] * n_in,
        out_specs=[VMEM] * len(outs),
        out_shape=[jax.ShapeDtypeStruct(s, d) for s, d in outs],
        scratch_shapes=list(scratch),
        compiler_params=pltpu.CompilerParams(vmem_limit_bytes=56 * 2**20),
        name=name,
    )


def attend(pos, lens, queries, d_context, keep, recv):
    wide = pl.BlockSpec((1, 1, 512, 128), lambda m, p, n: (0, m, 0, 0))
    kv = pl.BlockSpec((1, 64, 256), lambda m, p, n: (m, 0, 0))
    return pl.pallas_call(
        attend_kernel,
        grid_spec=pltpu.PrefetchScalarGridSpec(
            num_scalar_prefetch=2,
            grid=(8,),
            in_specs=[wide, wide, kv, kv],
            out_specs=[wide, wide, kv, kv],
        ),
        out_shape=[jax.ShapeDtypeStruct((1, 8, 512, 128), BF)] * 2
        + [jax.ShapeDtypeStruct((8, 64, 256), BF)] * 2,
        name="attend",
    )(pos, lens, queries, d_context, keep, recv)


def total(parts):
    return functools.reduce(lambda p, q: p + q, [p.astype(F32) for p in parts]).astype(BF)


def shards(enc_final, enc_len, kv_weight, queries, d_context):
    section, mp = lax.axis_index("section"), lax.axis_index("mp")
    c = mp % 2
    pos = jnp.stack([section // 2, mp // 8, ((mp // 2) % 4) * 2 + section % 2, c]).astype(jnp.int32)
    first = c == 0

    lower, upper = enc_final[0, :64], enc_final[0, 64:]
    mine = jnp.where(first, lower, upper)
    other = shift(jnp.where(first, upper, lower), dc=1)
    states = jnp.where(first, jnp.concatenate([mine, other], 1), jnp.concatenate([other, mine], 1))

    w_own = kv_weight.reshape(16, 256, 256)
    w_par = shift(w_own, dc=1)

    line = [states] + [shift(states, dz=k) for k in range(1, 8)]
    line_a = jnp.stack([p[:32] for p in line])
    line_b = jnp.stack([p[32:] for p in line])
    far = (2, 1, 3)
    got_a = {0: line_a}
    got_b = {0: line_b}
    for k in far:
        got_a[k] = shift(line_a, dx=k)
        got_b[k] = shift(line_b, dy=k)
    plane_a = jnp.stack([got_a[k] for k in range(4)])
    plane_b = jnp.stack([got_b[k] for k in range(4)])
    got_a = {0: plane_a}
    got_b = {0: plane_b}
    for k in far:
        got_a[k] = shift(plane_a, dy=k)
        got_b[k] = shift(plane_b, dx=k)
    pieces = [got_a[k] for k in range(4)] + [got_b[k] for k in range(4)]

    half = ((8, 64, 256), BF)
    keep, send = whole(
        project_kernel, 10, [half, half], [pltpu.VMEM((512, 256), F32)] * 2, name="project"
    )(pos, *pieces, w_own, w_par)
    recv = shift(send, dc=1)
    context, query_grad, grad_keep, grad_send = attend(pos, enc_len, queries, d_context, keep, recv)
    grad_recv = shift(grad_send, dc=1)

    block = ((4, 8, 32, 256), BF)
    parts = whole(spread_kernel, 4, [block] * 8, name="spread")(pos, grad_keep, grad_recv, w_own, w_par)
    sum_a, sum_b = [parts[0]], [parts[4]]
    for k in far:
        sum_a.append(shift(parts[k], dy=k))
        sum_b.append(shift(parts[4 + k], dx=k))

    grad_own, grad_par = whole(
        weight_kernel, 10, [((16, 256, 256), F32), ((16, 256, 256), BF)], name="weight"
    )(pos, *pieces, grad_keep, grad_recv)
    grad_other = shift(grad_par, dc=1)
    weight_grad = (grad_own + grad_other.astype(F32)).astype(BF).reshape(1, 4096, 2, 128)

    slice_a = [total([p[k] for p in sum_a]) for k in range(4)]
    slice_b = [total([p[k] for p in sum_b]) for k in range(4)]
    sum_a, sum_b = [slice_a[0]], [slice_b[0]]
    for k in far:
        sum_a.append(shift(slice_a[k], dx=k))
        sum_b.append(shift(slice_b[k], dy=k))
    line = [
        jnp.concatenate([total([p[k] for p in sum_a]), total([p[k] for p in sum_b])], 0)
        for k in range(8)
    ]
    rows = total([line[0]] + [shift(line[k], dz=k) for k in range(1, 8)])
    own = jnp.where(first, rows[:, :128], rows[:, 128:])
    other = shift(jnp.where(first, rows[:, 128:], rows[:, :128]), dc=1)
    enc_grad = jnp.where(first, jnp.concatenate([own, other], 0), jnp.concatenate([other, own], 0))
    return context, query_grad, weight_grad, enc_grad[None]


def solution(mesh):
    return jax.shard_map(
        shards,
        mesh=mesh,
        in_specs=(
            P("section", None, "mp"),
            P(),
            P("section", None, None, "mp"),
            P("section", None, None, "mp"),
            P("section", None, None, "mp"),
        ),
        out_specs=(
            P("section", None, None, "mp"),
            P("section", None, None, "mp"),
            P("section", None, None, "mp"),
            P("section", None, "mp"),
        ),
        check_vma=False,
    )
```

```python
import functools

import jax
import jax.numpy as jnp
from jax import lax
from jax.experimental import pallas as pl
from jax.experimental.pallas import tpu as pltpu
from jax.sharding import PartitionSpec as P

HD = 64
AXES = ("section", "mp")
BF = jnp.bfloat16
F32 = jnp.float32


def coords(i):
    section, mp = divmod(i, 32)
    x, zl = divmod(section, 2)
    y, zh, c = mp // 8, (mp // 2) % 4, mp % 2
    return x, y, 2 * zh + zl, c


def index(x, y, z, c):
    return ((x % 4) * 2 + z % 2) * 32 + (y % 4) * 8 + ((z % 8) // 2) * 2 + c


def shift(value, dx=0, dy=0, dz=0, dc=0):
    pairs = []
    for i in range(256):
        x, y, z, c = coords(i)
        pairs.append((i, index(x + dx, y + dy, z + dz, c ^ dc)))
    return lax.ppermute(value, AXES, pairs)


def cross(value, k, along):
    pairs = []
    for i in range(256):
        x, y, z, c = coords(i)
        dx, dy = (k, 0) if c == along else (0, k)
        pairs.append((i, index(x + dx, y + dy, z, c)))
    return lax.ppermute(value, AXES, pairs)


def nt(a, b):
    return lax.dot_general(a, b, (((1,), (1,)), ((), ())), preferred_element_type=F32)


def nn(a, b):
    return lax.dot_general(a, b, (((1,), (0,)), ((), ())), preferred_element_type=F32)


def tn(a, b):
    return lax.dot_general(a, b, (((0,), (0,)), ((), ())), preferred_element_type=F32)


def fetch(src, dst, sems):
    copies = [pltpu.make_async_copy(s, d, sems.at[i]) for i, (s, d) in enumerate(zip(src, dst))]
    for copy in copies:
        copy.start()
    return copies


def states_block(stack, dy, zh, z, c):
    rows = []
    for dx in range(4):
        outer, inner = c * dy + (1 - c) * dx, c * dx + (1 - c) * dy
        for zl in range(2):
            dz = (z + 8 - (2 * zh + zl)) & 7
            rows.append(stack[outer, inner, dz])
    return jnp.concatenate(rows, axis=0)


def fetch_weight(w, dst, start, slot, sem):
    return pltpu.make_async_copy(
        w.at[pl.ds(start, 4)], dst.at[pl.ds(start, 4)], sem.at[slot]
    )


def project_kernel(which, last, pos, *refs):
    n = len(which)
    x, y, z, c = pos[0], pos[1], pos[2], pos[3]
    pieces, refs = refs[:n], refs[n:]
    w_own, w_par, refs = refs[0], refs[1], refs[2:]
    if last:
        before, keep, send, stack, wo, wp, acc, sems, wsems = refs
    else:
        acc, stack, wo, wp, sems, wsems = refs

    def rows(copy_of):
        return [(y + 4 - dy) & 3 for dy in copy_of]

    def weights(copy_of):
        copies = []
        for i, yy in enumerate(rows(copy_of)):
            copies.append(
                (
                    fetch_weight(w_own, wo, yy * 4, 2 * i, wsems),
                    fetch_weight(w_par, wp, yy * 4, 2 * i + 1, wsems),
                )
            )
        for pair in copies:
            for copy in pair:
                copy.start()
        return copies

    copies = fetch(pieces, [stack.at[i] for i in range(n)], sems)
    if last:
        acc[...] = before[...]

    def block(copy_of, first, height, dxs, source):
        started = weights(copy_of)
        for copy in copies:
            copy.wait()
        sums = None
        for i, dy in enumerate(copy_of):
            yy = (y + 4 - dy) & 3
            lhs = jnp.concatenate(
                [
                    jnp.concatenate(
                        [
                            source(dx, dy)[(z + 8 - (2 * zh + zl)) & 7]
                            for dx in dxs
                            for zl in range(2)
                        ],
                        axis=0,
                    )
                    for zh in range(4)
                ],
                axis=1,
            )
            for copy in started[i]:
                copy.wait()
            own = nn(lhs, wo[pl.ds(yy * 4, 4)].reshape(1024, 256))
            par = nn(lhs, wp[pl.ds(yy * 4, 4)].reshape(1024, 256))
            sums = (own, par) if sums is None else (sums[0] + own, sums[1] + par)
        own, par = sums
        if last:
            own += acc[first : first + height, :256]
            par += acc[first : first + height, 256:]
        acc[first : first + height, :256] = own
        acc[first : first + height, 256:] = par

    @pl.when(c == 0)
    def _():
        first = which[0] * 128
        if not last:
            acc[...] = jnp.zeros_like(acc)
        block(range(4), first, n * 128, which, lambda dx, dy: stack.at[which.index(dx), dy])

    @pl.when(c == 1)
    def _():
        block(which, 0, 512, range(4), lambda dx, dy: stack.at[which.index(dy), dx])

    if last:
        for dx in range(4):
            for zl in range(2):
                m = ((x + 4 - dx) & 3) * 2 + zl
                row = (dx * 2 + zl) * 64
                keep[m] = acc[row : row + 64, :256].astype(BF)
                send[m] = acc[row : row + 64, 256:].astype(BF)


def attend_kernel(pos, lens, q_ref, d_ref, keep_ref, recv_ref, ctx_ref, qg_ref, own_ref, part_ref):
    c = pos[3]
    q = q_ref[0, 0]
    d = d_ref[0, 0]
    kv = jnp.concatenate([keep_ref[0], recv_ref[0]], axis=0)
    k, v = kv[:, :128], kv[:, 128:]
    left = lax.broadcasted_iota(jnp.int32, (128, 128), 1) < HD
    top = lax.broadcasted_iota(jnp.int32, (128, 128), 0) < HD
    zero = jnp.zeros((128, 128), BF)

    def stack_heads(t):
        return jnp.concatenate([jnp.where(left, t, zero), jnp.where(left, zero, t)], axis=0)

    def stack_heads_t(t):
        tt = t.T
        return jnp.concatenate([jnp.where(top, tt, zero), jnp.where(top, zero, tt)], axis=1)

    k_rows, v_rows = stack_heads(k), stack_heads(v)
    k_cols, v_cols = stack_heads_t(k), stack_heads_t(v)
    factor = HD ** (-0.5)
    source = (lax.broadcasted_iota(jnp.int32, (128, 512), 0) + 64 * c) & 127
    valid = source < lens[pl.program_id(0)]
    scores = nt(k_rows, q)
    prob_grad = nt(v_rows, d)
    probs, score_grads = [], []
    for h in range(2):
        s = jnp.where(valid, scores[h * 128 : h * 128 + 128] * factor, -1e30)
        e = jnp.exp(s - jnp.max(s, axis=0, keepdims=True))
        p = e * (1.0 / jnp.sum(e, axis=0, keepdims=True))
        g = prob_grad[h * 128 : h * 128 + 128]
        score_grads.append((p * (g - jnp.sum(g * p, axis=0, keepdims=True)) * factor).astype(BF))
        probs.append(p.astype(BF))
    prob = jnp.concatenate(probs, axis=0)
    score_grad = jnp.concatenate(score_grads, axis=0)
    ctx_ref[0, 0] = nn(v_cols, prob).astype(BF).T
    qg_ref[0, 0] = nn(k_cols, score_grad).astype(BF).T
    vg = nn(prob, d)
    kg = nn(score_grad, q)
    kg = jnp.where(left, kg[:128], kg[128:]).astype(BF)
    vg = jnp.where(left, vg[:128], vg[128:]).astype(BF)
    own_ref[0, :, :128] = kg[:64]
    own_ref[0, :, 128:] = vg[:64]
    part_ref[0, :, :128] = kg[64:]
    part_ref[0, :, 128:] = vg[64:]


def spread_kernel(which, after, pos, g_own, g_par, w_own, w_par, *refs):
    n = len(which)
    refs = refs[after:]
    outs, (wo, wp, wsems) = refs[:n], refs[n:]
    x, y, z, c = pos[0], pos[1], pos[2], pos[3]

    def block(dys, dxs, target):
        started = []
        for i, dy in enumerate(dys):
            yy = (y + dy) & 3
            pair = (
                fetch_weight(w_own, wo, yy * 4, 2 * i, wsems),
                fetch_weight(w_par, wp, yy * 4, 2 * i + 1, wsems),
            )
            for copy in pair:
                copy.start()
            started.append(pair)
        order = [(dx, zl, ((x + dx) & 3) * 2 + zl) for dx in dxs for zl in range(2)]
        own = jnp.concatenate([g_own[m] for _, _, m in order], axis=0)
        par = jnp.concatenate([g_par[m] for _, _, m in order], axis=0)
        for i, dy in enumerate(dys):
            yy = (y + dy) & 3
            for copy in started[i]:
                copy.wait()
            t = nt(own, wo[pl.ds(yy * 4, 4)].reshape(1024, 256))
            t = (t + nt(par, wp[pl.ds(yy * 4, 4)].reshape(1024, 256))).astype(BF)
            for j, (dx, zl, _) in enumerate(order):
                for zh in range(4):
                    target(dx, dy)[(2 * zh + zl + 8 - z) & 7] = t[
                        j * 64 : j * 64 + 64, zh * 256 : zh * 256 + 256
                    ]

    @pl.when(c == 0)
    def _():
        block(range(4), which, lambda dx, dy: outs[which.index(dx)].at[dy])

    @pl.when(c == 1)
    def _():
        block(which, range(4), lambda dx, dy: outs[which.index(dy)].at[dx])


def weight_kernel(pos, p0, p1, p2, p3, g_own, g_par, _, own_ref, par_ref, stack, sems):
    x, y, z, c = pos[0], pos[1], pos[2], pos[3]
    copies = fetch([p0, p1, p2, p3], [stack.at[i] for i in range(4)], sems)
    order = [((x + 4 - dx) & 3) * 2 + zl for dx in range(4) for zl in range(2)]
    own = jnp.concatenate([g_own[m] for m in order], axis=0)
    par = jnp.concatenate([g_par[m] for m in order], axis=0)
    for copy in copies:
        copy.wait()

    def step(i, _):
        dy = i // 4
        zh = i & 3
        lhs = states_block(stack, dy, zh, z, c)
        f = ((y + 4 - dy) & 3) * 4 + zh
        own_ref[f] = tn(lhs, own)
        par_ref[f] = tn(lhs, par).astype(BF)
        return 0

    lax.fori_loop(0, 16, step, 0)


SMEM = pl.BlockSpec(memory_space=pltpu.SMEM)
VMEM = pl.BlockSpec(memory_space=pltpu.VMEM)
HBM = pl.BlockSpec(memory_space=pl.ANY)


def stack_of(n):
    return pltpu.VMEM((n, 4, 8, 64, 256), BF)


WEIGHT = pltpu.VMEM((16, 256, 256), BF)


def whole(kernel, ins, outs, out_specs, scratch):
    return pl.pallas_call(
        kernel,
        in_specs=[SMEM] + ins,
        out_specs=out_specs,
        out_shape=[jax.ShapeDtypeStruct(s, d) for s, d in outs],
        scratch_shapes=scratch,
        compiler_params=pltpu.CompilerParams(vmem_limit_bytes=56 * 2**20),
    )


def sems(n):
    return pltpu.SemaphoreType.DMA((n,))


def spread(which, pos, own, par, w_own, w_par, after):
    return whole(
        functools.partial(spread_kernel, which, len(after)),
        [VMEM] * 2 + [HBM] * (2 + len(after)),
        [((4, 8, 64, 256), BF)] * len(which),
        [VMEM] * len(which),
        [WEIGHT, WEIGHT, sems(8)],
    )(pos, own, par, w_own, w_par, *after)


def attend(pos, lens, queries, d_context, keep, recv):
    wide = pl.BlockSpec((1, 1, 512, 128), lambda m, p, n: (0, m, 0, 0))
    kv = pl.BlockSpec((1, 64, 256), lambda m, p, n: (m, 0, 0))
    return pl.pallas_call(
        attend_kernel,
        grid_spec=pltpu.PrefetchScalarGridSpec(
            num_scalar_prefetch=2,
            grid=(8,),
            in_specs=[wide, wide, kv, kv],
            out_specs=[wide, wide, kv, kv],
        ),
        out_shape=[jax.ShapeDtypeStruct((1, 8, 512, 128), BF)] * 2
        + [jax.ShapeDtypeStruct((8, 64, 256), BF)] * 2,
        name="attend",
    )(pos, lens, queries, d_context, keep, recv)


def total(parts):
    return functools.reduce(lambda p, q: p + q, [p.astype(F32) for p in parts]).astype(BF)


def shards(enc_final, enc_len, kv_weight, queries, d_context):
    section, mp = lax.axis_index("section"), lax.axis_index("mp")
    c = mp % 2
    pos = jnp.stack([section // 2, mp // 8, ((mp // 2) % 4) * 2 + section % 2, c]).astype(jnp.int32)
    first = c == 0

    lower, upper = enc_final[0, :64], enc_final[0, 64:]
    mine = jnp.where(first, lower, upper)
    other = shift(jnp.where(first, upper, lower), dc=1)
    states = jnp.where(first, jnp.concatenate([mine, other], 1), jnp.concatenate([other, mine], 1))

    w_own = kv_weight.reshape(16, 256, 256)
    w_par = shift(w_own, dc=1)

    far = (2, 1, 3)
    line = jnp.stack([states] + [shift(states, dz=k) for k in range(1, 8)])
    got = {0: line}
    for k in far:
        got[k] = cross(line, k, 1)
    plane = jnp.stack([got[k] for k in range(4)])
    got = {0: plane}
    for k in far:
        got[k] = cross(plane, k, 0)
    pieces = [got[k] for k in range(4)]

    half = ((8, 64, 256), BF)
    (acc,) = whole(
        functools.partial(project_kernel, (0,), False),
        [HBM] * 3,
        [((512, 512), F32)],
        [VMEM],
        [stack_of(1), WEIGHT, WEIGHT, sems(1), sems(8)],
    )(pos, plane, w_own, w_par)
    keep, send = whole(
        functools.partial(project_kernel, (1, 2, 3), True),
        [HBM] * 5 + [VMEM],
        [half, half],
        [VMEM] * 2,
        [stack_of(3), WEIGHT, WEIGHT, pltpu.VMEM((512, 512), F32), sems(3), sems(8)],
    )(pos, *pieces[1:], w_own, w_par, acc)
    recv = shift(send, dc=1)
    context, query_grad, grad_keep, grad_send = attend(pos, enc_len, queries, d_context, keep, recv)
    grad_recv = shift(grad_send, dc=1)

    (part_2,) = spread((2,), pos, grad_keep, grad_recv, w_own, w_par, ())
    got_2 = cross(part_2, 2, 0)
    part_1, part_3 = spread((1, 3), pos, grad_keep, grad_recv, w_own, w_par, (part_2,))
    got_1 = cross(part_1, 1, 0)
    got_3 = cross(part_3, 3, 0)
    (part_0,) = spread((0,), pos, grad_keep, grad_recv, w_own, w_par, (part_1,))
    got = [part_0, got_1, got_2, got_3]

    grad_own, grad_par = whole(
        weight_kernel,
        [HBM] * 4 + [VMEM] * 2 + [HBM],
        [((16, 256, 256), F32), ((16, 256, 256), BF)],
        [VMEM] * 2,
        [stack_of(4), sems(4)],
    )(pos, *pieces, grad_keep, grad_recv, part_0)
    grad_other = shift(grad_par, dc=1)
    weight_grad = (grad_own + grad_other.astype(F32)).astype(BF).reshape(1, 4096, 2, 128)

    parts = [total([p[k] for p in got]) for k in range(4)]
    got = [parts[0]] + [cross(parts[k], k, 1) for k in far]
    got[0], weight_grad = lax.optimization_barrier((got[0], weight_grad))
    line = [total([p[k] for p in got]) for k in range(8)]
    rows = total([line[0]] + [shift(line[k], dz=k) for k in range(1, 8)])
    own = jnp.where(first, rows[:, :128], rows[:, 128:])
    other = shift(jnp.where(first, rows[:, 128:], rows[:, :128]), dc=1)
    enc_grad = jnp.where(first, jnp.concatenate([own, other], 0), jnp.concatenate([other, own], 0))
    return context, query_grad, weight_grad, enc_grad[None]


def solution(mesh):
    return jax.shard_map(
        shards,
        mesh=mesh,
        in_specs=(
            P("section", None, "mp"),
            P(),
            P("section", None, None, "mp"),
            P("section", None, None, "mp"),
            P("section", None, None, "mp"),
        ),
        out_specs=(
            P("section", None, None, "mp"),
            P("section", None, None, "mp"),
            P("section", None, None, "mp"),
            P("section", None, "mp"),
        ),
        check_vma=False,
    )
```

```python
import functools
import math

import jax
import jax.numpy as jnp
from jax import lax
from jax.experimental import pallas as pl
from jax.experimental.pallas import tpu as pltpu
from jax.sharding import PartitionSpec as P

HD = 64
ATTEND = 2
AXES = ("section", "mp")
BF = jnp.bfloat16
F32 = jnp.float32


def coords(i):
    section, mp = divmod(i, 32)
    x, zl = divmod(section, 2)
    y, zh, c = mp // 8, (mp // 2) % 4, mp % 2
    return x, y, 2 * zh + zl, c


def index(x, y, z, c):
    return ((x % 4) * 2 + z % 2) * 32 + (y % 4) * 8 + ((z % 8) // 2) * 2 + c


def shift(value, dx=0, dy=0, dz=0, dc=0):
    pairs = []
    for i in range(256):
        x, y, z, c = coords(i)
        pairs.append((i, index(x + dx, y + dy, z + dz, c ^ dc)))
    return lax.ppermute(value, AXES, pairs)


def cross(value, k, along):
    pairs = []
    for i in range(256):
        x, y, z, c = coords(i)
        dx, dy = (k, 0) if c == along else (0, k)
        pairs.append((i, index(x + dx, y + dy, z, c)))
    return lax.ppermute(value, AXES, pairs)


def nt(a, b):
    return lax.dot_general(a, b, (((1,), (1,)), ((), ())), preferred_element_type=F32)


def nn(a, b):
    return lax.dot_general(a, b, (((1,), (0,)), ((), ())), preferred_element_type=F32)


def project_kernel(which, last, pos, *refs):
    n = len(which)
    x, y, z, c = pos[0], pos[1], pos[2], pos[3]
    pieces, refs = refs[:n], refs[n:]
    wo, wp, refs = refs[0], refs[1], refs[2:]
    if last:
        before, keep, send, acc = refs
    else:
        (acc,) = refs

    def block(dys, first, height, dxs, source):
        own, par = None, None
        for dy in dys:
            yy = (y + 4 - dy) & 3
            columns = []
            for zh in range(4):
                rows = [
                    source(dx, dy)[(z + 8 - (2 * zh + zl)) & 7] for dx in dxs for zl in range(2)
                ]
                columns.append(jnp.concatenate(rows, axis=0))
            lhs = jnp.concatenate(columns, axis=1)
            own_term = nn(lhs, wo[pl.ds(yy * 4, 4)].reshape(1024, 256))
            par_term = nn(lhs, wp[pl.ds(yy * 4, 4)].reshape(1024, 256))
            own = own_term if own is None else own + own_term
            par = par_term if par is None else par + par_term
        if last:
            own += before[first : first + height, :256]
            par += before[first : first + height, 256:]
        acc[first : first + height, :256] = own
        acc[first : first + height, 256:] = par

    @pl.when(c == 0)
    def _():
        first = which[0] * 128
        if last:
            acc[:first] = before[:first]
        else:
            acc[...] = jnp.zeros_like(acc)
        block(range(4), first, n * 128, which, lambda dx, dy: pieces[which.index(dx)].at[dy])

    @pl.when(c == 1)
    def _():
        block(which, 0, 512, range(4), lambda dx, dy: pieces[which.index(dy)].at[dx])

    if last:
        for dx in range(4):
            for zl in range(2):
                m = ((x + 4 - dx) & 3) * 2 + zl
                row = (dx * 2 + zl) * 64
                keep[m] = acc[row : row + 64, :256].astype(BF)
                send[m] = acc[row : row + 64, 256:].astype(BF)


def attend_kernel(pos, lens, q_ref, d_ref, keep_ref, recv_ref, ctx_ref, qg_ref, own_ref, part_ref):
    left = lax.broadcasted_iota(jnp.int32, (128, 128), 1) < HD
    top = lax.broadcasted_iota(jnp.int32, (128, 128), 0) < HD
    zero = jnp.zeros((128, 128), BF)
    source = (lax.broadcasted_iota(jnp.int32, (128, 512), 0) + 64 * pos[3]) & 127
    factor = HD ** (-0.5)

    def stack_heads(t):
        return jnp.concatenate([jnp.where(left, t, zero), jnp.where(left, zero, t)], axis=0)

    def stack_heads_t(t):
        tt = t.T
        return jnp.concatenate([jnp.where(top, tt, zero), jnp.where(top, zero, tt)], axis=1)

    products = []
    for j in range(ATTEND):
        kv = jnp.concatenate([keep_ref[j], recv_ref[j]], axis=0)
        k, v = kv[:, :128], kv[:, 128:]
        products.append((k, v, nt(stack_heads(k), q_ref[0, j]), nt(stack_heads(v), d_ref[0, j])))
    for j, (k, v, scores, prob_grad) in enumerate(products):
        valid = source < lens[pl.program_id(0) * ATTEND + j]
        probs, score_grads = [], []
        for h in range(2):
            s = jnp.where(valid, scores[h * 128 : h * 128 + 128], -1e30)
            e = jnp.exp2((s - jnp.max(s, axis=0, keepdims=True)) * (factor * math.log2(math.e)))
            p = e * (1.0 / jnp.sum(e, axis=0, keepdims=True))
            g = prob_grad[h * 128 : h * 128 + 128]
            score_grads.append((p * (g - jnp.sum(g * p, axis=0, keepdims=True))).astype(BF))
            probs.append(p.astype(BF))
        prob = jnp.concatenate(probs, axis=0)
        score_grad = jnp.concatenate(score_grads, axis=0)
        ctx_ref[0, j] = nn(stack_heads_t(v), prob).astype(BF).T
        qg_ref[0, j] = nn(stack_heads_t(k * jnp.asarray(factor, BF)), score_grad).astype(BF).T
        vg = nn(prob, d_ref[0, j])
        kg = nn(score_grad, q_ref[0, j]) * factor
        kg = jnp.where(left, kg[:128], kg[128:]).astype(BF)
        vg = jnp.where(left, vg[:128], vg[128:]).astype(BF)
        own_ref[j, :, :128] = kg[:64]
        own_ref[j, :, 128:] = vg[:64]
        part_ref[j, :, :128] = kg[64:]
        part_ref[j, :, 128:] = vg[64:]


def spread_kernel(which, after, pos, g_own, g_par, wo, wp, *refs):
    outs = refs[after:]
    x, y, z, c = pos[0], pos[1], pos[2], pos[3]

    def block(dys, dxs, target):
        order = [(dx, zl, ((x + dx) & 3) * 2 + zl) for dx in dxs for zl in range(2)]
        own = jnp.concatenate([g_own[m] for _, _, m in order], axis=0)
        par = jnp.concatenate([g_par[m] for _, _, m in order], axis=0)
        for dy in dys:
            yy = (y + dy) & 3
            t = nt(own, wo[pl.ds(yy * 4, 4)].reshape(1024, 256))
            t = (t + nt(par, wp[pl.ds(yy * 4, 4)].reshape(1024, 256))).astype(BF)
            for j, (dx, zl, _) in enumerate(order):
                for zh in range(4):
                    target(dx, dy)[(2 * zh + zl + 8 - z) & 7] = t[
                        j * 64 : j * 64 + 64, zh * 256 : zh * 256 + 256
                    ]

    @pl.when(c == 0)
    def _():
        block(range(4), which, lambda dx, dy: outs[which.index(dx)].at[dy])

    @pl.when(c == 1)
    def _():
        block(which, range(4), lambda dx, dy: outs[which.index(dy)].at[dx])


def weight_kernel(pos, p0, p1, p2, p3, g_own, g_par, _, own_ref, par_ref):
    x, y, z, c = pos[0], pos[1], pos[2], pos[3]
    pieces = [p0, p1, p2, p3]
    order = [((x + 4 - dx) & 3) * 2 + zl for dx in range(4) for zl in range(2)]
    own = jnp.concatenate([g_own[m] for m in order], axis=0)
    par = jnp.concatenate([g_par[m] for m in order], axis=0)
    grads = jnp.concatenate([own, par], axis=1).T

    def product(block_of):
        for dy in range(4):
            yy = (y + 4 - dy) & 3

            def step(zh, _):
                rows = [
                    block_of(dx, dy)[(z + 8 - (2 * zh + zl)) & 7]
                    for dx in range(4)
                    for zl in range(2)
                ]
                out = nn(grads, jnp.concatenate(rows, axis=0)).astype(BF).T
                own_ref[yy * 4 + zh] = out[:, :256]
                par_ref[yy * 4 + zh] = out[:, 256:]
                return 0

            lax.fori_loop(0, 4, step, 0)

    @pl.when(c == 0)
    def _():
        product(lambda dx, dy: pieces[dx].at[dy])

    @pl.when(c == 1)
    def _():
        product(lambda dx, dy: pieces[dy].at[dx])


SMEM = pl.BlockSpec(memory_space=pltpu.SMEM)
VMEM = pl.BlockSpec(memory_space=pltpu.VMEM)
HBM = pl.BlockSpec(memory_space=pl.ANY)


def whole(kernel, ins, outs, out_specs, scratch):
    return pl.pallas_call(
        kernel,
        in_specs=[SMEM] + ins,
        out_specs=out_specs,
        out_shape=[jax.ShapeDtypeStruct(s, d) for s, d in outs],
        scratch_shapes=scratch,
        compiler_params=pltpu.CompilerParams(vmem_limit_bytes=20 * 2**20),
    )


def spread(which, pos, own, par, w_own, w_par, after):
    return whole(
        functools.partial(spread_kernel, which, len(after)),
        [VMEM] * 4 + [HBM] * len(after),
        [((4, 8, 64, 256), BF)] * len(which),
        [VMEM] * len(which),
        [],
    )(pos, own, par, w_own, w_par, *after)


def attend(pos, lens, queries, d_context, keep, recv):
    wide = pl.BlockSpec((1, ATTEND, 512, 128), lambda m, p, n: (0, m, 0, 0))
    kv = pl.BlockSpec((ATTEND, 64, 256), lambda m, p, n: (m, 0, 0))
    return pl.pallas_call(
        attend_kernel,
        grid_spec=pltpu.PrefetchScalarGridSpec(
            num_scalar_prefetch=2,
            grid=(8 // ATTEND,),
            in_specs=[wide, wide, kv, kv],
            out_specs=[wide, wide, kv, kv],
        ),
        out_shape=[jax.ShapeDtypeStruct((1, 8, 512, 128), BF)] * 2
        + [jax.ShapeDtypeStruct((8, 64, 256), BF)] * 2,
        compiler_params=pltpu.CompilerParams(vmem_limit_bytes=24 * 2**20),
        name="attend",
    )(pos, lens, queries, d_context, keep, recv)


def total(parts):
    return functools.reduce(lambda p, q: p + q, [p.astype(F32) for p in parts]).astype(BF)


def shards(enc_final, enc_len, kv_weight, queries, d_context):
    section, mp = lax.axis_index("section"), lax.axis_index("mp")
    c = mp % 2
    pos = jnp.stack([section // 2, mp // 8, ((mp // 2) % 4) * 2 + section % 2, c]).astype(jnp.int32)
    first = c == 0

    lower, upper = enc_final[0, :64], enc_final[0, 64:]
    mine = jnp.where(first, lower, upper)
    other = shift(jnp.where(first, upper, lower), dc=1)
    states = jnp.where(first, jnp.concatenate([mine, other], 1), jnp.concatenate([other, mine], 1))

    w_own = kv_weight.reshape(16, 256, 256)
    w_par = shift(w_own, dc=1)

    far = (2, 1, 3)
    line = jnp.stack([states] + [shift(states, dz=k) for k in range(1, 8)])
    got = {0: line}
    for k in far:
        got[k] = cross(line, k, 1)
    plane = jnp.stack([got[k] for k in range(4)])
    got = {0: plane}
    for k in far:
        got[k] = cross(plane, k, 0)
    pieces = [got[k] for k in range(4)]

    half = ((8, 64, 256), BF)
    (acc,) = whole(
        functools.partial(project_kernel, (0,), False), [VMEM] * 3, [((512, 512), F32)], [VMEM], []
    )(pos, plane, w_own, w_par)
    keep, send = whole(
        functools.partial(project_kernel, (1, 2, 3), True),
        [VMEM] * 6,
        [half, half],
        [VMEM] * 2,
        [pltpu.VMEM((512, 512), F32)],
    )(pos, *pieces[1:], w_own, w_par, acc)
    recv = shift(send, dc=1)
    context, query_grad, grad_keep, grad_send = attend(pos, enc_len, queries, d_context, keep, recv)
    grad_recv = shift(grad_send, dc=1)

    part_1, part_2, part_3 = spread((1, 2, 3), pos, grad_keep, grad_recv, w_own, w_par, ())
    got_1 = cross(part_1, 1, 0)
    got_2 = cross(part_2, 2, 0)
    got_3 = cross(part_3, 3, 0)
    (part_0,) = spread((0,), pos, grad_keep, grad_recv, w_own, w_par, (part_1,))
    got = [part_0, got_1, got_2, got_3]

    grad_own, grad_par = whole(
        weight_kernel, [VMEM] * 6 + [HBM], [((16, 256, 256), BF)] * 2, [VMEM] * 2, []
    )(pos, *pieces, grad_keep, grad_recv, part_0)
    grad_other = shift(grad_par, dc=1)
    weight_grad = total([grad_own, grad_other]).reshape(1, 4096, 2, 128)

    parts = [total([p[k] for p in got]) for k in range(4)]
    got = [parts[0]] + [cross(parts[k], k, 1) for k in far]
    got[0], weight_grad = lax.optimization_barrier((got[0], weight_grad))
    line = [total([p[k] for p in got]) for k in range(8)]
    rows = total([line[0]] + [shift(line[k], dz=k) for k in range(1, 8)])
    own = jnp.where(first, rows[:, :128], rows[:, 128:])
    other = shift(jnp.where(first, rows[:, 128:], rows[:, :128]), dc=1)
    enc_grad = jnp.where(first, jnp.concatenate([own, other], 0), jnp.concatenate([other, own], 0))
    return context, query_grad, weight_grad, enc_grad[None]


def solution(mesh):
    return jax.shard_map(
        shards,
        mesh=mesh,
        in_specs=(
            P("section", None, "mp"),
            P(),
            P("section", None, None, "mp"),
            P("section", None, None, "mp"),
            P("section", None, None, "mp"),
        ),
        out_specs=(
            P("section", None, None, "mp"),
            P("section", None, None, "mp"),
            P("section", None, None, "mp"),
            P("section", None, "mp"),
        ),
        check_vma=False,
    )
```

```python
import functools
import math

import jax
import jax.numpy as jnp
from jax import lax
from jax.experimental import pallas as pl
from jax.experimental.pallas import tpu as pltpu
from jax.sharding import PartitionSpec as P

HD = 64
ATTEND = 2
AXES = ("section", "mp")
BF = jnp.bfloat16
F32 = jnp.float32


def coords(i):
    section, mp = divmod(i, 32)
    x, zl = divmod(section, 2)
    y, zh, c = mp // 8, (mp // 2) % 4, mp % 2
    return x, y, 2 * zh + zl, c


def index(x, y, z, c):
    return ((x % 4) * 2 + z % 2) * 32 + (y % 4) * 8 + ((z % 8) // 2) * 2 + c


def shift(value, dx=0, dy=0, dz=0, dc=0):
    pairs = []
    for i in range(256):
        x, y, z, c = coords(i)
        pairs.append((i, index(x + dx, y + dy, z + dz, c ^ dc)))
    return lax.ppermute(value, AXES, pairs)


def cross(value, k, along):
    pairs = []
    for i in range(256):
        x, y, z, c = coords(i)
        dx, dy = (k, 0) if c == along else (0, k)
        pairs.append((i, index(x + dx, y + dy, z, c)))
    return lax.ppermute(value, AXES, pairs)


def rise(value, k):
    pairs = []
    for i in range(256):
        x, y, z, c = coords(i)
        pairs.append((i, index(x, y, z - k if c else z + k, c)))
    return lax.ppermute(value, AXES, pairs)


def nt(a, b):
    return lax.dot_general(a, b, (((1,), (1,)), ((), ())), preferred_element_type=F32)


def nn(a, b):
    return lax.dot_general(a, b, (((1,), (0,)), ((), ())), preferred_element_type=F32)


def slot_of(c, z, zh, zl):
    return ((1 - 2 * c) * (z - (2 * zh + zl)) + 16) & 7


def project_kernel(which, first, last, pos, *refs):
    n = len(which)
    x, y, z, c = pos[0], pos[1], pos[2], pos[3]
    pieces, (wo, wp), refs = refs[: 2 * n], refs[2 * n : 2 * n + 2], refs[2 * n + 2 :]
    if not first:
        before, refs = refs[0], refs[1:]
    acc = refs[-1]

    def piece(outer, inner):
        return pieces[2 * which.index(outer) + inner // 2].at[inner % 2]

    def product(dys, dxs, source):
        own, par = None, None
        for dy in dys:
            yy = (y + 4 - dy) & 3
            columns = []
            for zh in range(4):
                rows = [source(dx, dy)[slot_of(c, z, zh, zl)] for dx in dxs for zl in range(2)]
                columns.append(jnp.concatenate(rows, axis=0))
            lhs = jnp.concatenate(columns, axis=1)
            own_term = nn(lhs, wo[pl.ds(yy * 4, 4)].reshape(1024, 256))
            par_term = nn(lhs, wp[pl.ds(yy * 4, 4)].reshape(1024, 256))
            own = own_term if own is None else own + own_term
            par = par_term if par is None else par + par_term
        return own, par

    @pl.when(c == 0)
    def _():
        own, par = product(range(4), which, piece)
        for dx in range(4):
            to = slice(dx * 128, dx * 128 + 128)
            if dx in which:
                at = which.index(dx) * 128
                acc[to, :256] = own[at : at + 128]
                acc[to, 256:] = par[at : at + 128]
            elif not first:
                acc[to] = before[to]

    @pl.when(c == 1)
    def _():
        own, par = product(which, range(4), lambda dx, dy: piece(dy, dx))
        if first:
            acc[:, :256] = own
            acc[:, 256:] = par
        else:
            acc[:, :256] = own + before[:, :256]
            acc[:, 256:] = par + before[:, 256:]

    if last:
        keep, send = refs[0], refs[1]
        for dx in range(4):
            for zl in range(2):
                m = ((x + 4 - dx) & 3) * 2 + zl
                row = (dx * 2 + zl) * 64
                keep[m] = acc[row : row + 64, :256].astype(BF)
                send[m] = acc[row : row + 64, 256:].astype(BF)


def attend_kernel(pos, lens, q_ref, d_ref, keep_ref, recv_ref, ctx_ref, qg_ref, own_ref, part_ref):
    left = lax.broadcasted_iota(jnp.int32, (128, 128), 1) < HD
    top = lax.broadcasted_iota(jnp.int32, (128, 128), 0) < HD
    zero = jnp.zeros((128, 128), BF)
    source = (lax.broadcasted_iota(jnp.int32, (128, 512), 0) + 64 * pos[3]) & 127
    factor = HD ** (-0.5)

    def stack_heads(t):
        return jnp.concatenate([jnp.where(left, t, zero), jnp.where(left, zero, t)], axis=0)

    def stack_heads_t(t):
        tt = t.T
        return jnp.concatenate([jnp.where(top, tt, zero), jnp.where(top, zero, tt)], axis=1)

    products = []
    for j in range(ATTEND):
        kv = jnp.concatenate([keep_ref[j], recv_ref[j]], axis=0)
        k, v = kv[:, :128], kv[:, 128:]
        products.append((k, v, nt(stack_heads(k), q_ref[0, j]), nt(stack_heads(v), d_ref[0, j])))
    for j, (k, v, scores, prob_grad) in enumerate(products):
        valid = source < lens[pl.program_id(0) * ATTEND + j]
        probs, score_grads = [], []
        for h in range(2):
            s = jnp.where(valid, scores[h * 128 : h * 128 + 128], -1e30)
            e = jnp.exp2((s - jnp.max(s, axis=0, keepdims=True)) * (factor * math.log2(math.e)))
            p = e * (1.0 / jnp.sum(e, axis=0, keepdims=True))
            g = prob_grad[h * 128 : h * 128 + 128]
            score_grads.append((p * (g - jnp.sum(g * p, axis=0, keepdims=True))).astype(BF))
            probs.append(p.astype(BF))
        prob = jnp.concatenate(probs, axis=0)
        score_grad = jnp.concatenate(score_grads, axis=0)
        ctx_ref[0, j] = nn(stack_heads_t(v), prob).astype(BF).T
        qg_ref[0, j] = nn(stack_heads_t(k * jnp.asarray(factor, BF)), score_grad).astype(BF).T
        vg = nn(prob, d_ref[0, j])
        kg = nn(score_grad, q_ref[0, j]) * factor
        kg = jnp.where(left, kg[:128], kg[128:]).astype(BF)
        vg = jnp.where(left, vg[:128], vg[128:]).astype(BF)
        own_ref[j, :, :128] = kg[:64]
        own_ref[j, :, 128:] = vg[:64]
        part_ref[j, :, :128] = kg[64:]
        part_ref[j, :, 128:] = vg[64:]


def spread_kernel(which, after, pos, g_own, g_par, wo, wp, *refs):
    outs = refs[after:]
    x, y, z, c = pos[0], pos[1], pos[2], pos[3]

    def product(dxs):
        order = [((x + dx) & 3) * 2 + zl for dx in dxs for zl in range(2)]
        own = jnp.concatenate([g_own[m] for m in order], axis=0)
        par = jnp.concatenate([g_par[m] for m in order], axis=0)

        def emit(dy, target):
            yy = (y + dy) & 3
            t = nt(own, wo[pl.ds(yy * 4, 4)].reshape(1024, 256))
            t = (t + nt(par, wp[pl.ds(yy * 4, 4)].reshape(1024, 256))).astype(BF)
            for i, dx in enumerate(dxs):
                for zl in range(2):
                    row = i * 128 + zl * 64
                    for zh in range(4):
                        target(dx)[slot_of(1 - c, z, zh, zl)] = t[
                            row : row + 64, zh * 256 : zh * 256 + 256
                        ]

        return emit

    @pl.when(c == 0)
    def _():
        emit = product(which)
        for half in range(2):

            def step(inner, _):
                emit(2 * half + inner, lambda dx: outs[2 * which.index(dx) + half].at[inner])
                return 0

            lax.fori_loop(0, 2, step, 0)

    @pl.when(c == 1)
    def _():
        emit = product(range(4))
        for i, dy in enumerate(which):
            emit(dy, lambda dx: outs[2 * i + dx // 2].at[dx % 2])


def weight_kernel(pos, *refs):
    pieces, (g_own, g_par, _, own_ref, par_ref) = refs[:8], refs[8:]
    x, y, z, c = pos[0], pos[1], pos[2], pos[3]
    order = [((x + 4 - dx) & 3) * 2 + zl for dx in range(4) for zl in range(2)]
    own = jnp.concatenate([g_own[m] for m in order], axis=0)
    par = jnp.concatenate([g_par[m] for m in order], axis=0)
    grads = jnp.concatenate([own, par], axis=1).T

    def emit(dy, zh, source):
        rows = [source(dx)[slot_of(c, z, zh, zl)] for dx in range(4) for zl in range(2)]
        out = nn(grads, jnp.concatenate(rows, axis=0)).astype(BF).T
        f = ((y + 4 - dy) & 3) * 4 + zh
        own_ref[f] = out[:, :256]
        par_ref[f] = out[:, 256:]

    @pl.when(c == 0)
    def _():
        for half in range(2):

            def step(i, _):
                inner = i // 4
                emit(2 * half + inner, i & 3, lambda dx: pieces[2 * dx + half].at[inner])
                return 0

            lax.fori_loop(0, 8, step, 0)

    @pl.when(c == 1)
    def _():
        for dy in range(4):

            def step(zh, _):
                emit(dy, zh, lambda dx: pieces[2 * dy + dx // 2].at[dx % 2])
                return 0

            lax.fori_loop(0, 4, step, 0)


SMEM = pl.BlockSpec(memory_space=pltpu.SMEM)
VMEM = pl.BlockSpec(memory_space=pltpu.VMEM)
HBM = pl.BlockSpec(memory_space=pl.ANY)


def whole(kernel, ins, outs, out_specs, scratch):
    return pl.pallas_call(
        kernel,
        in_specs=[SMEM] + ins,
        out_specs=out_specs,
        out_shape=[jax.ShapeDtypeStruct(s, d) for s, d in outs],
        scratch_shapes=scratch,
        compiler_params=pltpu.CompilerParams(vmem_limit_bytes=20 * 2**20),
    )


def project(which, pos, pieces, w_own, w_par, before, last):
    first = before is None
    acc = ((512, 512), F32)
    half = ((8, 64, 256), BF)
    return whole(
        functools.partial(project_kernel, which, first, last),
        [VMEM] * (2 * len(which) + (2 if first else 3)),
        [half, half] if last else [acc],
        [VMEM] * (2 if last else 1),
        [pltpu.VMEM((512, 512), F32)] if last else [],
    )(pos, *pieces, w_own, w_par, *([] if first else [before]))


def spread(which, pos, own, par, w_own, w_par, after):
    return whole(
        functools.partial(spread_kernel, which, len(after)),
        [VMEM] * 4 + [HBM] * len(after),
        [((2, 8, 64, 256), BF)] * (2 * len(which)),
        [VMEM] * (2 * len(which)),
        [],
    )(pos, own, par, w_own, w_par, *after)


def attend(pos, lens, queries, d_context, keep, recv):
    wide = pl.BlockSpec((1, ATTEND, 512, 128), lambda m, p, n: (0, m, 0, 0))
    kv = pl.BlockSpec((ATTEND, 64, 256), lambda m, p, n: (m, 0, 0))
    return pl.pallas_call(
        attend_kernel,
        grid_spec=pltpu.PrefetchScalarGridSpec(
            num_scalar_prefetch=2,
            grid=(8 // ATTEND,),
            in_specs=[wide, wide, kv, kv],
            out_specs=[wide, wide, kv, kv],
        ),
        out_shape=[jax.ShapeDtypeStruct((1, 8, 512, 128), BF)] * 2
        + [jax.ShapeDtypeStruct((8, 64, 256), BF)] * 2,
        compiler_params=pltpu.CompilerParams(vmem_limit_bytes=24 * 2**20),
        name="attend",
    )(pos, lens, queries, d_context, keep, recv)


def total(parts):
    return functools.reduce(lambda p, q: p + q, [p.astype(F32) for p in parts]).astype(BF)


def shards(enc_final, enc_len, kv_weight, queries, d_context):
    section, mp = lax.axis_index("section"), lax.axis_index("mp")
    c = mp % 2
    pos = jnp.stack([section // 2, mp // 8, ((mp // 2) % 4) * 2 + section % 2, c]).astype(jnp.int32)
    first = c == 0

    local = enc_final[0]
    other = shift(local, dc=1)
    states = jnp.where(
        first, jnp.concatenate([local, other], 1), jnp.concatenate([other, local], 1)
    ).reshape(2, 64, 256)

    def halves(v, axis):
        lower, upper = lax.index_in_dim(v, 0, axis, False), lax.index_in_dim(v, 1, axis, False)
        return jnp.where(first, lower, upper), jnp.where(first, upper, lower)

    mine, _ = halves(states, 0)
    across = shift(mine, dz=4)
    got = []
    for k in (3, 2, 1):
        got.append(rise(states, k))
    near, passed = halves(jnp.stack(got), 1)
    passed = shift(passed, dc=1)
    line = jnp.concatenate([mine[None], near[::-1], across[None], passed], 0)

    w_own = kv_weight.reshape(16, 256, 256)
    w_par = shift(w_own, dc=1)

    slices = {0: line}
    for k in (1, 3, 2):
        slices[k] = cross(line, k, 1)
    low = jnp.stack([slices[0], slices[1]])
    high = jnp.stack([slices[2], slices[3]])
    right_low = cross(low, 1, 0)
    left_low = cross(low, 3, 0)
    left_high = cross(high, 3, 0)
    right_high = cross(high, 1, 0)
    far_low = cross(right_low, 1, 0)
    far_high = cross(left_high, 3, 0)
    near = (right_low, right_high, left_low, left_high)

    (acc,) = project((0,), pos, (low, high), w_own, w_par, None, False)
    (acc,) = project((1, 3), pos, near, w_own, w_par, acc, False)
    keep, send = project((2,), pos, (far_low, far_high), w_own, w_par, acc, True)
    recv = shift(send, dc=1)
    context, query_grad, grad_keep, grad_send = attend(pos, enc_len, queries, d_context, keep, recv)
    grad_recv = shift(grad_send, dc=1)

    right_low_g, right_high_g, far_low_g, far_high_g, left_low_g, left_high_g = spread(
        (1, 2, 3), pos, grad_keep, grad_recv, w_own, w_par, ()
    )
    pass_low = cross(far_low_g, 1, 0)
    pass_high = cross(far_high_g, 3, 0)
    from_left_high = cross(right_high_g, 1, 0)
    from_right_low = cross(left_low_g, 3, 0)
    own_low, own_high = spread(
        (0,), pos, grad_keep, grad_recv, w_own, w_par, (right_low_g,)
    )
    from_left_low = cross(total([right_low_g, pass_low]), 1, 0)
    from_right_high = cross(total([left_high_g, pass_high]), 3, 0)

    grad_own, grad_par = whole(
        weight_kernel, [VMEM] * 10 + [HBM], [((16, 256, 256), BF)] * 2, [VMEM] * 2, []
    )(pos, low, high, right_low, right_high, far_low, far_high, left_low, left_high, grad_keep, grad_recv, own_low)
    grad_other = shift(grad_par, dc=1)
    weight_grad = total([grad_own, grad_other]).reshape(1, 4096, 2, 128)

    low = [total([own_low[k], from_left_low[k], from_right_low[k]]) for k in range(2)]
    high = [total([own_high[k], from_left_high[k], from_right_high[k]]) for k in range(2)]
    got = [low[0]]
    for k in (1, 3, 2):
        got.append(cross((low + high)[k], k, 1))
    got[0], weight_grad = lax.optimization_barrier((got[0], weight_grad))
    passed = [total([p[8 - k] for p in got]) for k in (3, 2, 1)]
    passed = shift(jnp.stack(passed), dc=1)
    across = shift(total([p[4] for p in got]), dz=4)
    got_z = []
    for i, k in enumerate((3, 2, 1)):
        both = jnp.stack([total([p[k] for p in got]), passed[i]])
        got_z.append(rise(both, k).astype(F32))
    both = got_z[0] + got_z[1] + got_z[2]
    mine = functools.reduce(lambda p, q: p + q, [p[0].astype(F32) for p in got])
    both = jnp.stack([both[0] + mine + across.astype(F32), both[1]]).reshape(2, 64, 2, 128)
    kept, passed = halves(both, 2)
    passed = shift(passed.astype(BF), dc=1).astype(F32)
    kept, far_half = (kept[0] + passed[1]).astype(BF), (kept[1] + passed[0]).astype(BF)
    enc_grad = jnp.where(
        first, jnp.concatenate([kept, far_half], 0), jnp.concatenate([far_half, kept], 0)
    )
    return context, query_grad, weight_grad, enc_grad[None]


def solution(mesh):
    return jax.shard_map(
        shards,
        mesh=mesh,
        in_specs=(
            P("section", None, "mp"),
            P(),
            P("section", None, None, "mp"),
            P("section", None, None, "mp"),
            P("section", None, None, "mp"),
        ),
        out_specs=(
            P("section", None, None, "mp"),
            P("section", None, None, "mp"),
            P("section", None, None, "mp"),
            P("section", None, "mp"),
        ),
        check_vma=False,
    )
```

```python
import functools
import math

import jax
import jax.numpy as jnp
from jax import lax
from jax.experimental import pallas as pl
from jax.experimental.pallas import tpu as pltpu
from jax.sharding import PartitionSpec as P

HD = 64
ATTEND = 2
AXES = ("section", "mp")
BF = jnp.bfloat16
F32 = jnp.float32


def coords(i):
    section, mp = divmod(i, 32)
    x, zl = divmod(section, 2)
    y, zh, c = mp // 8, (mp // 2) % 4, mp % 2
    return x, y, 2 * zh + zl, c


def index(x, y, z, c):
    return ((x % 4) * 2 + z % 2) * 32 + (y % 4) * 8 + ((z % 8) // 2) * 2 + c


def shift(value, dx=0, dy=0, dz=0, dc=0):
    pairs = []
    for i in range(256):
        x, y, z, c = coords(i)
        pairs.append((i, index(x + dx, y + dy, z + dz, c ^ dc)))
    return lax.ppermute(value, AXES, pairs)


def cross(value, k, along):
    pairs = []
    for i in range(256):
        x, y, z, c = coords(i)
        dx, dy = (k, 0) if c == along else (0, k)
        pairs.append((i, index(x + dx, y + dy, z, c)))
    return lax.ppermute(value, AXES, pairs)


def rise(value, k):
    pairs = []
    for i in range(256):
        x, y, z, c = coords(i)
        pairs.append((i, index(x, y, z - k if c else z + k, c)))
    return lax.ppermute(value, AXES, pairs)


def nt(a, b):
    return lax.dot_general(a, b, (((1,), (1,)), ((), ())), preferred_element_type=F32)


def nn(a, b):
    return lax.dot_general(a, b, (((1,), (0,)), ((), ())), preferred_element_type=F32)


def slot_of(c, z, zh, zl):
    return ((1 - 2 * c) * (z - (2 * zh + zl)) + 16) & 7


def project_kernel(which, first, last, pos, *refs):
    n = len(which)
    x, y, z, c = pos[0], pos[1], pos[2], pos[3]
    pieces, (wo, wp), refs = refs[: 2 * n], refs[2 * n : 2 * n + 2], refs[2 * n + 2 :]
    if first:
        refs[0][...] = wp[...]
    else:
        before, refs = refs[0], refs[1:]
    acc = refs[-1]

    def product(dy, dxs, source):
        f = ((y + 4 - dy) & 3) * 4
        columns = []
        for zh in range(4):
            rows = [source(dx)[slot_of(c, z, zh, zl)] for dx in dxs for zl in range(2)]
            columns.append(jnp.concatenate(rows, axis=0))
        lhs = jnp.concatenate(columns, axis=1)
        own = nn(lhs, wo[pl.ds(f, 4)].reshape(1024, 256))
        return own, nn(lhs, wp[pl.ds(f, 4)].reshape(1024, 256))

    @pl.when(c == 0)
    def _():
        for dx in range(4):
            to = slice(dx * 128, dx * 128 + 128)
            if dx in which or first:
                acc[to] = jnp.zeros((128, 512), F32)
            else:
                acc[to] = before[to]
        for half in range(2):

            def step(inner, _):
                own, par = product(
                    2 * half + inner,
                    which,
                    lambda dx: pieces[2 * which.index(dx) + half].at[inner],
                )
                for i, dx in enumerate(which):
                    acc[dx * 128 : dx * 128 + 128, :256] += own[i * 128 : i * 128 + 128]
                    acc[dx * 128 : dx * 128 + 128, 256:] += par[i * 128 : i * 128 + 128]
                return 0

            lax.fori_loop(0, 2, step, 0)

    @pl.when(c == 1)
    def _():
        own, par = None, None
        for i, dy in enumerate(which):
            own_term, par_term = product(
                dy, range(4), lambda dx: pieces[2 * i + dx // 2].at[dx % 2]
            )
            own = own_term if own is None else own + own_term
            par = par_term if par is None else par + par_term
        if first:
            acc[:, :256] = own
            acc[:, 256:] = par
        else:
            acc[:, :256] = own + before[:, :256]
            acc[:, 256:] = par + before[:, 256:]

    if last:
        keep, send = refs[0], refs[1]
        for dx in range(4):
            for zl in range(2):
                m = ((x + 4 - dx) & 3) * 2 + zl
                row = (dx * 2 + zl) * 64
                keep[m] = acc[row : row + 64, :256].astype(BF)
                send[m] = acc[row : row + 64, 256:].astype(BF)


def attend_kernel(pos, lens, q_ref, d_ref, keep_ref, recv_ref, ctx_ref, qg_ref, own_ref, part_ref):
    left = lax.broadcasted_iota(jnp.int32, (128, 128), 1) < HD
    top = lax.broadcasted_iota(jnp.int32, (128, 128), 0) < HD
    zero = jnp.zeros((128, 128), BF)
    source = (lax.broadcasted_iota(jnp.int32, (128, 512), 0) + 64 * pos[3]) & 127
    factor = HD ** (-0.5)

    def stack_heads(t):
        return jnp.concatenate([jnp.where(left, t, zero), jnp.where(left, zero, t)], axis=0)

    def stack_heads_t(t):
        tt = t.T
        return jnp.concatenate([jnp.where(top, tt, zero), jnp.where(top, zero, tt)], axis=1)

    products = []
    for j in range(ATTEND):
        kv = jnp.concatenate([keep_ref[j], recv_ref[j]], axis=0)
        k, v = kv[:, :128], kv[:, 128:]
        products.append((k, v, nt(stack_heads(k), q_ref[0, j]), nt(stack_heads(v), d_ref[0, j])))
    for j, (k, v, scores, prob_grad) in enumerate(products):
        valid = source < lens[pl.program_id(0) * ATTEND + j]
        probs, score_grads = [], []
        for h in range(2):
            s = jnp.where(valid, scores[h * 128 : h * 128 + 128], -1e30)
            e = jnp.exp2((s - jnp.max(s, axis=0, keepdims=True)) * (factor * math.log2(math.e)))
            p = e * (1.0 / jnp.sum(e, axis=0, keepdims=True))
            g = prob_grad[h * 128 : h * 128 + 128]
            score_grads.append((p * (g - jnp.sum(g * p, axis=0, keepdims=True))).astype(BF))
            probs.append(p.astype(BF))
        prob = jnp.concatenate(probs, axis=0)
        score_grad = jnp.concatenate(score_grads, axis=0)
        ctx_ref[0, j] = nn(stack_heads_t(v), prob).astype(BF).T
        qg_ref[0, j] = nn(stack_heads_t(k * jnp.asarray(factor, BF)), score_grad).astype(BF).T
        vg = nn(prob, d_ref[0, j])
        kg = nn(score_grad, q_ref[0, j]) * factor
        kg = jnp.where(left, kg[:128], kg[128:]).astype(BF)
        vg = jnp.where(left, vg[:128], vg[128:]).astype(BF)
        own_ref[j, :, :128] = kg[:64]
        own_ref[j, :, 128:] = vg[:64]
        part_ref[j, :, :128] = kg[64:]
        part_ref[j, :, 128:] = vg[64:]


def spread_kernel(which, after, pos, g_own, g_par, wo, wp, *refs):
    outs = refs[after:]
    x, y, z, c = pos[0], pos[1], pos[2], pos[3]

    def product(dxs):
        order = [((x + dx) & 3) * 2 + zl for dx in dxs for zl in range(2)]
        own = jnp.concatenate([g_own[m] for m in order], axis=0)
        par = jnp.concatenate([g_par[m] for m in order], axis=0)

        def emit(dy, target):
            yy = (y + dy) & 3
            t = nt(own, wo[pl.ds(yy * 4, 4)].reshape(1024, 256))
            t = (t + nt(par, wp[pl.ds(yy * 4, 4)].reshape(1024, 256))).astype(BF)
            for i, dx in enumerate(dxs):
                for zl in range(2):
                    row = i * 128 + zl * 64
                    for zh in range(4):
                        target(dx)[slot_of(1 - c, z, zh, zl)] = t[
                            row : row + 64, zh * 256 : zh * 256 + 256
                        ]

        return emit

    @pl.when(c == 0)
    def _():
        emit = product(which)
        for half in range(2):

            def step(inner, _):
                emit(2 * half + inner, lambda dx: outs[2 * which.index(dx) + half].at[inner])
                return 0

            lax.fori_loop(0, 2, step, 0)

    @pl.when(c == 1)
    def _():
        emit = product(range(4))
        for i, dy in enumerate(which):
            emit(dy, lambda dx: outs[2 * i + dx // 2].at[dx % 2])


def weight_kernel(pos, *refs):
    pieces, (g_own, g_par, _, own_ref, par_ref) = refs[:8], refs[8:]
    x, y, z, c = pos[0], pos[1], pos[2], pos[3]
    order = [((x + 4 - dx) & 3) * 2 + zl for dx in range(4) for zl in range(2)]
    own = jnp.concatenate([g_own[m] for m in order], axis=0)
    par = jnp.concatenate([g_par[m] for m in order], axis=0)
    grads = jnp.concatenate([own, par], axis=1).T

    def emit(dy, zh, source):
        rows = [source(dx)[slot_of(c, z, zh, zl)] for dx in range(4) for zl in range(2)]
        out = nn(grads, jnp.concatenate(rows, axis=0)).astype(BF).T
        f = ((y + 4 - dy) & 3) * 4 + zh
        own_ref[f] = out[:, :256]
        par_ref[f] = out[:, 256:]

    @pl.when(c == 0)
    def _():
        for half in range(2):

            def step(i, _):
                inner = i // 4
                emit(2 * half + inner, i & 3, lambda dx: pieces[2 * dx + half].at[inner])
                return 0

            lax.fori_loop(0, 8, step, 0)

    @pl.when(c == 1)
    def _():
        for dy in range(4):

            def step(zh, _):
                emit(dy, zh, lambda dx: pieces[2 * dy + dx // 2].at[dx % 2])
                return 0

            lax.fori_loop(0, 4, step, 0)


SMEM = pl.BlockSpec(memory_space=pltpu.SMEM)
VMEM = pl.BlockSpec(memory_space=pltpu.VMEM)
HBM = pl.BlockSpec(memory_space=pl.ANY)


def whole(kernel, ins, outs, out_specs, scratch):
    return pl.pallas_call(
        kernel,
        in_specs=[SMEM] + ins,
        out_specs=out_specs,
        out_shape=[jax.ShapeDtypeStruct(s, d) for s, d in outs],
        scratch_shapes=scratch,
        compiler_params=pltpu.CompilerParams(vmem_limit_bytes=20 * 2**20),
    )


def project(which, pos, pieces, w_own, w_par, before, last):
    first = before is None
    acc = ((512, 512), F32)
    half = ((8, 64, 256), BF)
    outs = [half, half] if last else [acc]
    if first:
        outs = [((16, 256, 256), BF), acc]
    return whole(
        functools.partial(project_kernel, which, first, last),
        [VMEM] * (2 * len(which) + (2 if first else 3)),
        outs,
        [VMEM] * len(outs),
        [pltpu.VMEM((512, 512), F32)] if last else [],
    )(pos, *pieces, w_own, w_par, *([] if first else [before]))


def spread(which, pos, own, par, w_own, w_par, after):
    return whole(
        functools.partial(spread_kernel, which, len(after)),
        [VMEM] * 4 + [HBM] * len(after),
        [((2, 8, 64, 256), BF)] * (2 * len(which)),
        [VMEM] * (2 * len(which)),
        [],
    )(pos, own, par, w_own, w_par, *after)


def attend(pos, lens, queries, d_context, keep, recv):
    wide = pl.BlockSpec((1, ATTEND, 512, 128), lambda m, p, n: (0, m, 0, 0))
    kv = pl.BlockSpec((ATTEND, 64, 256), lambda m, p, n: (m, 0, 0))
    return pl.pallas_call(
        attend_kernel,
        grid_spec=pltpu.PrefetchScalarGridSpec(
            num_scalar_prefetch=2,
            grid=(8 // ATTEND,),
            in_specs=[wide, wide, kv, kv],
            out_specs=[wide, wide, kv, kv],
        ),
        out_shape=[jax.ShapeDtypeStruct((1, 8, 512, 128), BF)] * 2
        + [jax.ShapeDtypeStruct((8, 64, 256), BF)] * 2,
        compiler_params=pltpu.CompilerParams(vmem_limit_bytes=24 * 2**20),
        name="attend",
    )(pos, lens, queries, d_context, keep, recv)


def total(parts):
    return functools.reduce(lambda p, q: p + q, [p.astype(F32) for p in parts]).astype(BF)


def shards(enc_final, enc_len, kv_weight, queries, d_context):
    section, mp = lax.axis_index("section"), lax.axis_index("mp")
    c = mp % 2
    pos = jnp.stack([section // 2, mp // 8, ((mp // 2) % 4) * 2 + section % 2, c]).astype(jnp.int32)
    first = c == 0

    local = enc_final[0]
    other = shift(local, dc=1)
    states = jnp.where(
        first, jnp.concatenate([local, other], 1), jnp.concatenate([other, local], 1)
    ).reshape(2, 64, 256)

    def halves(v, axis):
        lower, upper = lax.index_in_dim(v, 0, axis, False), lax.index_in_dim(v, 1, axis, False)
        return jnp.where(first, lower, upper), jnp.where(first, upper, lower)

    mine, _ = halves(states, 0)
    across = shift(mine, dz=4)
    got = []
    for k in (3, 2, 1):
        got.append(rise(states, k))
    near, passed = halves(jnp.stack(got), 1)
    passed = shift(passed, dc=1)
    line = jnp.concatenate([mine[None], near[::-1], across[None], passed], 0)

    w_own = kv_weight.reshape(16, 256, 256)
    w_par = shift(w_own, dc=1)

    slices = {0: line}
    for k in (1, 3, 2):
        slices[k] = cross(line, k, 1)
    low = jnp.stack([slices[0], slices[1]])
    high = jnp.stack([slices[2], slices[3]])
    right_low = cross(low, 1, 0)
    left_low = cross(low, 3, 0)
    left_high = cross(high, 3, 0)
    right_high = cross(high, 1, 0)
    far_low = cross(right_low, 1, 0)
    far_high = cross(left_high, 3, 0)
    near = (right_low, right_high, left_low, left_high)

    w_par, acc = project((0,), pos, (low, high), w_own, w_par, None, False)
    (acc,) = project((1, 3), pos, near, w_own, w_par, acc, False)
    keep, send = project((2,), pos, (far_low, far_high), w_own, w_par, acc, True)
    recv = shift(send, dc=1)
    context, query_grad, grad_keep, grad_send = attend(pos, enc_len, queries, d_context, keep, recv)
    grad_recv = shift(grad_send, dc=1)

    far_low_g, far_high_g = spread((2,), pos, grad_keep, grad_recv, w_own, w_par, ())
    pass_low = cross(far_low_g, 1, 0)
    pass_high = cross(far_high_g, 3, 0)
    right_low_g, right_high_g, left_low_g, left_high_g = spread(
        (1, 3), pos, grad_keep, grad_recv, w_own, w_par, (far_low_g,)
    )
    from_left_high = cross(right_high_g, 1, 0)
    from_right_low = cross(left_low_g, 3, 0)
    own_low, own_high = spread(
        (0,), pos, grad_keep, grad_recv, w_own, w_par, (right_low_g,)
    )
    from_left_low = cross(total([right_low_g, pass_low]), 1, 0)
    from_right_high = cross(total([left_high_g, pass_high]), 3, 0)

    grad_own, grad_par = whole(
        weight_kernel, [VMEM] * 10 + [HBM], [((16, 256, 256), BF)] * 2, [VMEM] * 2, []
    )(pos, low, high, right_low, right_high, far_low, far_high, left_low, left_high, grad_keep, grad_recv, own_low)
    grad_other = shift(grad_par, dc=1)
    weight_grad = total([grad_own, grad_other]).reshape(1, 4096, 2, 128)

    low = [total([own_low[k], from_left_low[k], from_right_low[k]]) for k in range(2)]
    high = [total([own_high[k], from_left_high[k], from_right_high[k]]) for k in range(2)]
    got = [low[0]]
    for k in (1, 3, 2):
        got.append(cross((low + high)[k], k, 1))
    got[0], weight_grad = lax.optimization_barrier((got[0], weight_grad))
    passed = [total([p[8 - k] for p in got]) for k in (3, 2, 1)]
    passed = shift(jnp.stack(passed), dc=1)
    across = shift(total([p[4] for p in got]), dz=4)
    got_z = []
    for i, k in enumerate((3, 2, 1)):
        both = jnp.stack([total([p[k] for p in got]), passed[i]])
        got_z.append(rise(both, k).astype(F32))
    both = got_z[0] + got_z[1] + got_z[2]
    mine = functools.reduce(lambda p, q: p + q, [p[0].astype(F32) for p in got])
    both = jnp.stack([both[0] + mine + across.astype(F32), both[1]]).reshape(2, 64, 2, 128)
    kept, passed = halves(both, 2)
    passed = shift(passed.astype(BF), dc=1).astype(F32)
    kept, far_half = (kept[0] + passed[1]).astype(BF), (kept[1] + passed[0]).astype(BF)
    enc_grad = jnp.where(
        first, jnp.concatenate([kept, far_half], 0), jnp.concatenate([far_half, kept], 0)
    )
    return context, query_grad, weight_grad, enc_grad[None]


def solution(mesh):
    return jax.shard_map(
        shards,
        mesh=mesh,
        in_specs=(
            P("section", None, "mp"),
            P(),
            P("section", None, None, "mp"),
            P("section", None, None, "mp"),
            P("section", None, None, "mp"),
        ),
        out_specs=(
            P("section", None, None, "mp"),
            P("section", None, None, "mp"),
            P("section", None, None, "mp"),
            P("section", None, "mp"),
        ),
        check_vma=False,
    )
```

```python
import functools
import math

import jax
import jax.numpy as jnp
from jax import lax
from jax.experimental import pallas as pl
from jax.experimental.pallas import tpu as pltpu
from jax.sharding import PartitionSpec as P

HD = 64
ATTEND = 2
AXES = ("section", "mp")
BF = jnp.bfloat16
F32 = jnp.float32


def coords(i):
    section, mp = divmod(i, 32)
    x, zl = divmod(section, 2)
    y, zh, c = mp // 8, (mp // 2) % 4, mp % 2
    return x, y, 2 * zh + zl, c


def index(x, y, z, c):
    return ((x % 4) * 2 + z % 2) * 32 + (y % 4) * 8 + ((z % 8) // 2) * 2 + c


def shift(value, dx=0, dy=0, dz=0, dc=0):
    pairs = []
    for i in range(256):
        x, y, z, c = coords(i)
        pairs.append((i, index(x + dx, y + dy, z + dz, c ^ dc)))
    return lax.ppermute(value, AXES, pairs)


def cross(value, k, along):
    pairs = []
    for i in range(256):
        x, y, z, c = coords(i)
        dx, dy = (k, 0) if c == along else (0, k)
        pairs.append((i, index(x + dx, y + dy, z, c)))
    return lax.ppermute(value, AXES, pairs)


def rise(value, k):
    pairs = []
    for i in range(256):
        x, y, z, c = coords(i)
        pairs.append((i, index(x, y, z - k if c else z + k, c)))
    return lax.ppermute(value, AXES, pairs)


def nt(a, b):
    return lax.dot_general(a, b, (((1,), (1,)), ((), ())), preferred_element_type=F32)


def nn(a, b):
    return lax.dot_general(a, b, (((1,), (0,)), ((), ())), preferred_element_type=F32)


def slot_of(c, z, zh, zl):
    return ((1 - 2 * c) * (z - (2 * zh + zl)) + 16) & 7


def project_kernel(which, first, last, pos, *refs):
    n = len(which)
    x, y, z, c = pos[0], pos[1], pos[2], pos[3]
    pieces, (wo, wp), refs = refs[: 2 * n], refs[2 * n : 2 * n + 2], refs[2 * n + 2 :]
    if first:
        refs[0][...] = wp[...]
    else:
        before, refs = refs[0], refs[1:]
    acc = refs[-1]

    def product(dy, dxs, source):
        f = ((y + 4 - dy) & 3) * 4
        columns = []
        for zh in range(4):
            rows = [source(dx)[slot_of(c, z, zh, zl)] for dx in dxs for zl in range(2)]
            columns.append(jnp.concatenate(rows, axis=0))
        lhs = jnp.concatenate(columns, axis=1)
        own = nn(lhs, wo[pl.ds(f, 4)].reshape(1024, 256))
        return own, nn(lhs, wp[pl.ds(f, 4)].reshape(1024, 256))

    @pl.when(c == 0)
    def _():
        for dx in range(4):
            to = slice(dx * 128, dx * 128 + 128)
            if dx in which or first:
                acc[to] = jnp.zeros((128, 512), F32)
            else:
                acc[to] = before[to]
        for half in range(2):

            def step(inner, _):
                own, par = product(
                    2 * half + inner,
                    which,
                    lambda dx: pieces[2 * which.index(dx) + half].at[inner],
                )
                for i, dx in enumerate(which):
                    acc[dx * 128 : dx * 128 + 128, :256] += own[i * 128 : i * 128 + 128]
                    acc[dx * 128 : dx * 128 + 128, 256:] += par[i * 128 : i * 128 + 128]
                return 0

            lax.fori_loop(0, 2, step, 0)

    @pl.when(c == 1)
    def _():
        own, par = None, None
        for i, dy in enumerate(which):
            own_term, par_term = product(
                dy, range(4), lambda dx: pieces[2 * i + dx // 2].at[dx % 2]
            )
            own = own_term if own is None else own + own_term
            par = par_term if par is None else par + par_term
        if first:
            acc[:, :256] = own
            acc[:, 256:] = par
        else:
            acc[:, :256] = own + before[:, :256]
            acc[:, 256:] = par + before[:, 256:]

    if last:
        keep, send = refs[0], refs[1]
        for dx in range(4):
            for zl in range(2):
                m = ((x + 4 - dx) & 3) * 2 + zl
                row = (dx * 2 + zl) * 64
                keep[m] = acc[row : row + 64, :256].astype(BF)
                send[m] = acc[row : row + 64, 256:].astype(BF)


def attend_kernel(pos, lens, q_ref, d_ref, keep_ref, recv_ref, ctx_ref, qg_ref, own_ref, part_ref):
    left = lax.broadcasted_iota(jnp.int32, (128, 128), 1) < HD
    top = lax.broadcasted_iota(jnp.int32, (128, 128), 0) < HD
    zero = jnp.zeros((128, 128), BF)
    source = (lax.broadcasted_iota(jnp.int32, (128, 512), 0) + 64 * pos[3]) & 127
    factor = HD ** (-0.5)

    def stack_heads(t):
        return jnp.concatenate([jnp.where(left, t, zero), jnp.where(left, zero, t)], axis=0)

    def stack_heads_t(t):
        tt = t.T
        return jnp.concatenate([jnp.where(top, tt, zero), jnp.where(top, zero, tt)], axis=1)

    products = []
    for j in range(ATTEND):
        kv = jnp.concatenate([keep_ref[j], recv_ref[j]], axis=0)
        k, v = kv[:, :128], kv[:, 128:]
        products.append((k, v, nt(stack_heads(k), q_ref[0, j]), nt(stack_heads(v), d_ref[0, j])))
    for j, (k, v, scores, prob_grad) in enumerate(products):
        valid = source < lens[pl.program_id(0) * ATTEND + j]
        probs, score_grads = [], []
        for h in range(2):
            s = jnp.where(valid, scores[h * 128 : h * 128 + 128], -1e30)
            e = jnp.exp2((s - jnp.max(s, axis=0, keepdims=True)) * (factor * math.log2(math.e)))
            p = e * (1.0 / jnp.sum(e, axis=0, keepdims=True))
            g = prob_grad[h * 128 : h * 128 + 128]
            score_grads.append((p * (g - jnp.sum(g * p, axis=0, keepdims=True))).astype(BF))
            probs.append(p.astype(BF))
        prob = jnp.concatenate(probs, axis=0)
        score_grad = jnp.concatenate(score_grads, axis=0)
        ctx_ref[0, j] = nn(stack_heads_t(v), prob).astype(BF).T
        qg_ref[0, j] = nn(stack_heads_t(k * jnp.asarray(factor, BF)), score_grad).astype(BF).T
        vg = nn(prob, d_ref[0, j])
        kg = nn(score_grad, q_ref[0, j]) * factor
        kg = jnp.where(left, kg[:128], kg[128:]).astype(BF)
        vg = jnp.where(left, vg[:128], vg[128:]).astype(BF)
        own_ref[j, :, :128] = kg[:64]
        own_ref[j, :, 128:] = vg[:64]
        part_ref[j, :, :128] = kg[64:]
        part_ref[j, :, 128:] = vg[64:]


def spread_kernel(which, after, pos, g_own, g_par, wo, wp, *refs):
    outs = refs[after:]
    x, y, z, c = pos[0], pos[1], pos[2], pos[3]

    def product(dxs):
        order = [((x + dx) & 3) * 2 + zl for dx in dxs for zl in range(2)]
        own = jnp.concatenate([g_own[m] for m in order], axis=0)
        par = jnp.concatenate([g_par[m] for m in order], axis=0)

        def emit(dy, target):
            yy = (y + dy) & 3
            t = nt(own, wo[pl.ds(yy * 4, 4)].reshape(1024, 256))
            t = (t + nt(par, wp[pl.ds(yy * 4, 4)].reshape(1024, 256))).astype(BF)
            for i, dx in enumerate(dxs):
                for zl in range(2):
                    row = i * 128 + zl * 64
                    for zh in range(4):
                        target(dx)[slot_of(1 - c, z, zh, zl)] = t[
                            row : row + 64, zh * 256 : zh * 256 + 256
                        ]

        return emit

    @pl.when(c == 0)
    def _():
        emit = product(which)
        for half in range(2):

            def step(inner, _):
                emit(2 * half + inner, lambda dx: outs[2 * which.index(dx) + half].at[inner])
                return 0

            lax.fori_loop(0, 2, step, 0)

    @pl.when(c == 1)
    def _():
        emit = product(range(4))
        for i, dy in enumerate(which):
            emit(dy, lambda dx: outs[2 * i + dx // 2].at[dx % 2])


def weight_kernel(half, pos, *refs):
    pieces, (g_own, g_par) = refs[:8], refs[8:10]
    own_ref, par_ref = refs[-2:]
    x, y, z, c = pos[0], pos[1], pos[2], pos[3]
    order = [((x + 4 - dx) & 3) * 2 + zl for dx in range(4) for zl in range(2)]
    own = jnp.concatenate([g_own[m] for m in order], axis=0)
    par = jnp.concatenate([g_par[m] for m in order], axis=0)
    grads = jnp.concatenate([own, par], axis=1).T

    def emit(dy, zh, source):
        rows = [source(dx)[slot_of(c, z, zh, zl)] for dx in range(4) for zl in range(2)]
        out = nn(grads, jnp.concatenate(rows, axis=0)).astype(BF).T
        f = ((y + 4 - dy) & 3) * 4 + zh
        own_ref[f] = out[:, :256]
        par_ref[f] = out[:, 256:]

    @pl.when(c == 0)
    def _():
        def step(i, _):
            inner = i // 4
            emit(2 * half + inner, i & 3, lambda dx: pieces[2 * dx + half].at[inner])
            return 0

        lax.fori_loop(0, 8, step, 0)

    @pl.when(c == 1)
    def _():
        for dy in (2 * half, 2 * half + 1):

            def step(zh, _):
                emit(dy, zh, lambda dx: pieces[2 * dy + dx // 2].at[dx % 2])
                return 0

            lax.fori_loop(0, 4, step, 0)


SMEM = pl.BlockSpec(memory_space=pltpu.SMEM)
VMEM = pl.BlockSpec(memory_space=pltpu.VMEM)
HBM = pl.BlockSpec(memory_space=pl.ANY)


def whole(kernel, ins, outs, out_specs, scratch, aliases=None):
    return pl.pallas_call(
        kernel,
        in_specs=[SMEM] + ins,
        out_specs=out_specs,
        out_shape=[jax.ShapeDtypeStruct(s, d) for s, d in outs],
        scratch_shapes=scratch,
        input_output_aliases=aliases or {},
        compiler_params=pltpu.CompilerParams(vmem_limit_bytes=20 * 2**20),
    )


def project(which, pos, pieces, w_own, w_par, before, last):
    first = before is None
    acc = ((512, 512), F32)
    half = ((8, 64, 256), BF)
    outs = [half, half] if last else [acc]
    if first:
        outs = [((16, 256, 256), BF), acc]
    return whole(
        functools.partial(project_kernel, which, first, last),
        [VMEM] * (2 * len(which) + (2 if first else 3)),
        outs,
        [VMEM] * len(outs),
        [pltpu.VMEM((512, 512), F32)] if last else [],
    )(pos, *pieces, w_own, w_par, *([] if first else [before]))


def spread(which, pos, own, par, w_own, w_par, after):
    return whole(
        functools.partial(spread_kernel, which, len(after)),
        [VMEM] * 4 + [HBM] * len(after),
        [((2, 8, 64, 256), BF)] * (2 * len(which)),
        [VMEM] * (2 * len(which)),
        [],
    )(pos, own, par, w_own, w_par, *after)


def attend(pos, lens, queries, d_context, keep, recv):
    wide = pl.BlockSpec((1, ATTEND, 512, 128), lambda m, p, n: (0, m, 0, 0))
    kv = pl.BlockSpec((ATTEND, 64, 256), lambda m, p, n: (m, 0, 0))
    return pl.pallas_call(
        attend_kernel,
        grid_spec=pltpu.PrefetchScalarGridSpec(
            num_scalar_prefetch=2,
            grid=(8 // ATTEND,),
            in_specs=[wide, wide, kv, kv],
            out_specs=[wide, wide, kv, kv],
        ),
        out_shape=[jax.ShapeDtypeStruct((1, 8, 512, 128), BF)] * 2
        + [jax.ShapeDtypeStruct((8, 64, 256), BF)] * 2,
        compiler_params=pltpu.CompilerParams(vmem_limit_bytes=24 * 2**20),
        name="attend",
    )(pos, lens, queries, d_context, keep, recv)


def total(parts):
    return functools.reduce(lambda p, q: p + q, [p.astype(F32) for p in parts]).astype(BF)


def shards(enc_final, enc_len, kv_weight, queries, d_context):
    section, mp = lax.axis_index("section"), lax.axis_index("mp")
    c = mp % 2
    pos = jnp.stack([section // 2, mp // 8, ((mp // 2) % 4) * 2 + section % 2, c]).astype(jnp.int32)
    first = c == 0

    local = enc_final[0]
    other = shift(local, dc=1)
    states = jnp.where(
        first, jnp.concatenate([local, other], 1), jnp.concatenate([other, local], 1)
    ).reshape(2, 64, 256)

    def halves(v, axis):
        lower, upper = lax.index_in_dim(v, 0, axis, False), lax.index_in_dim(v, 1, axis, False)
        return jnp.where(first, lower, upper), jnp.where(first, upper, lower)

    mine, _ = halves(states, 0)
    across = shift(mine, dz=4)
    got = []
    for k in (3, 2, 1):
        got.append(rise(states, k))
    near, passed = halves(jnp.stack(got), 1)
    passed = shift(passed, dc=1)
    line = jnp.concatenate([mine[None], near[::-1], across[None], passed], 0)

    w_own = kv_weight.reshape(16, 256, 256)
    w_par = shift(w_own, dc=1)

    slices = {0: line}
    for k in (1, 3, 2):
        slices[k] = cross(line, k, 1)
    low = jnp.stack([slices[0], slices[1]])
    high = jnp.stack([slices[2], slices[3]])
    right_low = cross(low, 1, 0)
    left_low = cross(low, 3, 0)
    left_high = cross(high, 3, 0)
    right_high = cross(high, 1, 0)
    far_low = cross(right_low, 1, 0)
    far_high = cross(left_high, 3, 0)
    near = (right_low, right_high, left_low, left_high)

    w_par, acc = project((0,), pos, (low, high), w_own, w_par, None, False)
    (acc,) = project((1, 3), pos, near, w_own, w_par, acc, False)
    keep, send = project((2,), pos, (far_low, far_high), w_own, w_par, acc, True)
    recv = shift(send, dc=1)
    context, query_grad, grad_keep, grad_send = attend(pos, enc_len, queries, d_context, keep, recv)
    grad_recv = shift(grad_send, dc=1)

    far_low_g, far_high_g = spread((2,), pos, grad_keep, grad_recv, w_own, w_par, ())
    pass_low = cross(far_low_g, 1, 0)
    pass_high = cross(far_high_g, 3, 0)
    right_low_g, right_high_g, left_low_g, left_high_g = spread(
        (1, 3), pos, grad_keep, grad_recv, w_own, w_par, (far_low_g,)
    )
    from_left_high = cross(right_high_g, 1, 0)
    from_right_low = cross(left_low_g, 3, 0)
    own_low, own_high = spread(
        (0,), pos, grad_keep, grad_recv, w_own, w_par, (right_low_g,)
    )
    from_left_low = cross(total([right_low_g, pass_low]), 1, 0)
    from_right_high = cross(total([left_high_g, pass_high]), 3, 0)

    states_in = (low, high, right_low, right_high, far_low, far_high, left_low, left_high)

    def weight(half, done):
        return whole(
            functools.partial(weight_kernel, half),
            [VMEM] * (10 + len(done)),
            [((16, 256, 256), BF)] * 2,
            [VMEM] * 2,
            [],
            {11: 0, 12: 1} if done else None,
        )(pos, *states_in, grad_keep, grad_recv, *done)

    grad_parts = weight(0, ())
    grad_own, grad_par = weight(1, grad_parts)
    grad_other = shift(grad_par, dc=1)
    weight_grad = total([grad_own, grad_other]).reshape(1, 4096, 2, 128)

    low = [total([own_low[k], from_left_low[k], from_right_low[k]]) for k in range(2)]
    high = [total([own_high[k], from_left_high[k], from_right_high[k]]) for k in range(2)]
    got = [low[0]]
    for k in (1, 3, 2):
        got.append(cross((low + high)[k], k, 1))
    passed = [total([p[8 - k] for p in got]) for k in (3, 2, 1)]
    passed = shift(jnp.stack(passed), dc=1)
    across = shift(total([p[4] for p in got]), dz=4)
    got_z = []
    for i, k in enumerate((3, 2, 1)):
        both = jnp.stack([total([p[k] for p in got]), passed[i]])
        got_z.append(rise(both, k).astype(F32))
    got_z[0], weight_grad = lax.optimization_barrier((got_z[0], weight_grad))
    both = got_z[0] + got_z[1] + got_z[2]
    mine = functools.reduce(lambda p, q: p + q, [p[0].astype(F32) for p in got])
    both = jnp.stack([both[0] + mine + across.astype(F32), both[1]]).reshape(2, 64, 2, 128)
    kept, passed = halves(both, 2)
    passed = shift(passed.astype(BF), dc=1).astype(F32)
    kept, far_half = (kept[0] + passed[1]).astype(BF), (kept[1] + passed[0]).astype(BF)
    enc_grad = jnp.where(
        first, jnp.concatenate([kept, far_half], 0), jnp.concatenate([far_half, kept], 0)
    )
    return context, query_grad, weight_grad, enc_grad[None]


def solution(mesh):
    return jax.shard_map(
        shards,
        mesh=mesh,
        in_specs=(
            P("section", None, "mp"),
            P(),
            P("section", None, None, "mp"),
            P("section", None, None, "mp"),
            P("section", None, None, "mp"),
        ),
        out_specs=(
            P("section", None, None, "mp"),
            P("section", None, None, "mp"),
            P("section", None, None, "mp"),
            P("section", None, "mp"),
        ),
        check_vma=False,
    )
```

```python
import functools
import math

import jax
import jax.numpy as jnp
from jax import lax
from jax.experimental import pallas as pl
from jax.experimental.pallas import tpu as pltpu
from jax.sharding import PartitionSpec as P

HD = 64
ATTEND = 2
AXES = ("section", "mp")
BF = jnp.bfloat16
F32 = jnp.float32


def coords(i):
    section, mp = divmod(i, 32)
    x, zl = divmod(section, 2)
    y, zh, c = mp // 8, (mp // 2) % 4, mp % 2
    return x, y, 2 * zh + zl, c


def index(x, y, z, c):
    return ((x % 4) * 2 + z % 2) * 32 + (y % 4) * 8 + ((z % 8) // 2) * 2 + c


def shift(value, dx=0, dy=0, dz=0, dc=0):
    pairs = []
    for i in range(256):
        x, y, z, c = coords(i)
        pairs.append((i, index(x + dx, y + dy, z + dz, c ^ dc)))
    return lax.ppermute(value, AXES, pairs)


def cross(value, k, along):
    pairs = []
    for i in range(256):
        x, y, z, c = coords(i)
        dx, dy = (k, 0) if c == along else (0, k)
        pairs.append((i, index(x + dx, y + dy, z, c)))
    return lax.ppermute(value, AXES, pairs)


def rise(value, k):
    pairs = []
    for i in range(256):
        x, y, z, c = coords(i)
        pairs.append((i, index(x, y, z - k if c else z + k, c)))
    return lax.ppermute(value, AXES, pairs)


def nt(a, b):
    return lax.dot_general(a, b, (((1,), (1,)), ((), ())), preferred_element_type=F32)


def nn(a, b):
    return lax.dot_general(a, b, (((1,), (0,)), ((), ())), preferred_element_type=F32)


def slot_of(c, z, zh, zl):
    return ((1 - 2 * c) * (z - (2 * zh + zl)) + 16) & 7


def project_kernel(which, first, last, pos, *refs):
    n = len(which)
    x, y, z, c = pos[0], pos[1], pos[2], pos[3]
    pieces, (wo, wp), refs = refs[: 2 * n], refs[2 * n : 2 * n + 2], refs[2 * n + 2 :]
    if first:
        refs[0][...] = wp[...]
    else:
        before, refs = refs[0], refs[1:]
    acc = refs[-1]

    def product(dy, dxs, source):
        f = ((y + 4 - dy) & 3) * 4
        columns = []
        for zh in range(4):
            rows = [source(dx)[slot_of(c, z, zh, zl)] for dx in dxs for zl in range(2)]
            columns.append(jnp.concatenate(rows, axis=0))
        lhs = jnp.concatenate(columns, axis=1)
        own = nn(lhs, wo[pl.ds(f, 4)].reshape(1024, 256))
        return own, nn(lhs, wp[pl.ds(f, 4)].reshape(1024, 256))

    @pl.when(c == 0)
    def _():
        for dx in range(4):
            to = slice(dx * 128, dx * 128 + 128)
            if dx in which or first:
                acc[to] = jnp.zeros((128, 512), F32)
            else:
                acc[to] = before[to]
        for half in range(2):

            def step(inner, _):
                own, par = product(
                    2 * half + inner,
                    which,
                    lambda dx: pieces[2 * which.index(dx) + half].at[inner],
                )
                for i, dx in enumerate(which):
                    acc[dx * 128 : dx * 128 + 128, :256] += own[i * 128 : i * 128 + 128]
                    acc[dx * 128 : dx * 128 + 128, 256:] += par[i * 128 : i * 128 + 128]
                return 0

            lax.fori_loop(0, 2, step, 0)

    @pl.when(c == 1)
    def _():
        own, par = None, None
        for i, dy in enumerate(which):
            own_term, par_term = product(
                dy, range(4), lambda dx: pieces[2 * i + dx // 2].at[dx % 2]
            )
            own = own_term if own is None else own + own_term
            par = par_term if par is None else par + par_term
        if first:
            acc[:, :256] = own
            acc[:, 256:] = par
        else:
            acc[:, :256] = own + before[:, :256]
            acc[:, 256:] = par + before[:, 256:]

    if last:
        keep, send = refs[0], refs[1]
        for dx in range(4):
            for zl in range(2):
                m = ((x + 4 - dx) & 3) * 2 + zl
                row = (dx * 2 + zl) * 64
                keep[m] = acc[row : row + 64, :256].astype(BF)
                send[m] = acc[row : row + 64, 256:].astype(BF)


def attend_kernel(pos, lens, q_ref, d_ref, keep_ref, recv_ref, ctx_ref, qg_ref, own_ref, part_ref):
    left = lax.broadcasted_iota(jnp.int32, (128, 128), 1) < HD
    top = lax.broadcasted_iota(jnp.int32, (128, 128), 0) < HD
    zero = jnp.zeros((128, 128), BF)
    source = (lax.broadcasted_iota(jnp.int32, (128, 512), 0) + 64 * pos[3]) & 127
    factor = HD ** (-0.5)

    def stack_heads(t):
        return jnp.concatenate([jnp.where(left, t, zero), jnp.where(left, zero, t)], axis=0)

    def stack_heads_t(t):
        tt = t.T
        return jnp.concatenate([jnp.where(top, tt, zero), jnp.where(top, zero, tt)], axis=1)

    products = []
    for j in range(ATTEND):
        kv = jnp.concatenate([keep_ref[j], recv_ref[j]], axis=0)
        k, v = kv[:, :128], kv[:, 128:]
        products.append((k, v, nt(stack_heads(k), q_ref[0, j]), nt(stack_heads(v), d_ref[0, j])))
    for j, (k, v, scores, prob_grad) in enumerate(products):
        valid = source < lens[pl.program_id(0) * ATTEND + j]
        probs, score_grads = [], []
        for h in range(2):
            s = jnp.where(valid, scores[h * 128 : h * 128 + 128], -1e30)
            e = jnp.exp2((s - jnp.max(s, axis=0, keepdims=True)) * (factor * math.log2(math.e)))
            p = e * (1.0 / jnp.sum(e, axis=0, keepdims=True))
            g = prob_grad[h * 128 : h * 128 + 128]
            score_grads.append((p * (g - jnp.sum(g * p, axis=0, keepdims=True))).astype(BF))
            probs.append(p.astype(BF))
        prob = jnp.concatenate(probs, axis=0)
        score_grad = jnp.concatenate(score_grads, axis=0)
        ctx_ref[0, j] = nn(stack_heads_t(v), prob).astype(BF).T
        qg_ref[0, j] = nn(stack_heads_t(k * jnp.asarray(factor, BF)), score_grad).astype(BF).T
        vg = nn(prob, d_ref[0, j])
        kg = nn(score_grad, q_ref[0, j]) * factor
        kg = jnp.where(left, kg[:128], kg[128:]).astype(BF)
        vg = jnp.where(left, vg[:128], vg[128:]).astype(BF)
        own_ref[j, :, :128] = kg[:64]
        own_ref[j, :, 128:] = vg[:64]
        part_ref[j, :, :128] = kg[64:]
        part_ref[j, :, 128:] = vg[64:]


def spread_kernel(which, after, pos, g_own, g_par, wo, wp, *refs):
    outs = refs[after:]
    x, y, z, c = pos[0], pos[1], pos[2], pos[3]

    def product(dxs):
        order = [((x + dx) & 3) * 2 + zl for dx in dxs for zl in range(2)]
        own = jnp.concatenate([g_own[m] for m in order], axis=0)
        par = jnp.concatenate([g_par[m] for m in order], axis=0)

        def emit(dy, target):
            yy = (y + dy) & 3
            t = nt(own, wo[pl.ds(yy * 4, 4)].reshape(1024, 256))
            t = (t + nt(par, wp[pl.ds(yy * 4, 4)].reshape(1024, 256))).astype(BF)
            for i, dx in enumerate(dxs):
                for zl in range(2):
                    row = i * 128 + zl * 64
                    for zh in range(4):
                        target(dx)[slot_of(1 - c, z, zh, zl)] = t[
                            row : row + 64, zh * 256 : zh * 256 + 256
                        ]

        return emit

    @pl.when(c == 0)
    def _():
        emit = product(which)
        for half in range(2):

            def step(inner, _):
                emit(2 * half + inner, lambda dx: outs[2 * which.index(dx) + half].at[inner])
                return 0

            lax.fori_loop(0, 2, step, 0)

    @pl.when(c == 1)
    def _():
        emit = product(range(4))
        for i, dy in enumerate(which):
            emit(dy, lambda dx: outs[2 * i + dx // 2].at[dx % 2])


def weight_kernel(pos, *refs):
    pieces, (g_own, g_par, own_ref, par_ref) = refs[:8], refs[8:]
    x, y, z, c = pos[0], pos[1], pos[2], pos[3]
    order = [((x + 4 - dx) & 3) * 2 + zl for dx in range(4) for zl in range(2)]
    own = jnp.concatenate([g_own[m] for m in order], axis=0)
    par = jnp.concatenate([g_par[m] for m in order], axis=0)
    grads = jnp.concatenate([own, par], axis=1).T

    def emit(dy, zh, source):
        rows = [source(dx)[slot_of(c, z, zh, zl)] for dx in range(4) for zl in range(2)]
        out = nn(grads, jnp.concatenate(rows, axis=0)).astype(BF).T
        f = ((y + 4 - dy) & 3) * 4 + zh
        own_ref[f] = out[:, :256]
        par_ref[f] = out[:, 256:]

    @pl.when(c == 0)
    def _():
        for half in range(2):

            def step(i, _):
                inner = i // 4
                emit(2 * half + inner, i & 3, lambda dx: pieces[2 * dx + half].at[inner])
                return 0

            lax.fori_loop(0, 8, step, 0)

    @pl.when(c == 1)
    def _():
        for dy in range(4):

            def step(zh, _):
                emit(dy, zh, lambda dx: pieces[2 * dy + dx // 2].at[dx % 2])
                return 0

            lax.fori_loop(0, 4, step, 0)


SMEM = pl.BlockSpec(memory_space=pltpu.SMEM)
VMEM = pl.BlockSpec(memory_space=pltpu.VMEM)
HBM = pl.BlockSpec(memory_space=pl.ANY)


def whole(kernel, ins, outs, out_specs, scratch):
    return pl.pallas_call(
        kernel,
        in_specs=[SMEM] + ins,
        out_specs=out_specs,
        out_shape=[jax.ShapeDtypeStruct(s, d) for s, d in outs],
        scratch_shapes=scratch,
        compiler_params=pltpu.CompilerParams(vmem_limit_bytes=12 * 2**20),
    )


def project(which, pos, pieces, w_own, w_par, before, last):
    first = before is None
    acc = ((512, 512), F32)
    half = ((8, 64, 256), BF)
    outs = [half, half] if last else [acc]
    if first:
        outs = [((16, 256, 256), BF), acc]
    return whole(
        functools.partial(project_kernel, which, first, last),
        [VMEM] * (2 * len(which) + (2 if first else 3)),
        outs,
        [VMEM] * len(outs),
        [pltpu.VMEM((512, 512), F32)] if last else [],
    )(pos, *pieces, w_own, w_par, *([] if first else [before]))


def spread(which, pos, own, par, w_own, w_par, after):
    return whole(
        functools.partial(spread_kernel, which, len(after)),
        [VMEM] * 4 + [HBM] * len(after),
        [((2, 8, 64, 256), BF)] * (2 * len(which)),
        [VMEM] * (2 * len(which)),
        [],
    )(pos, own, par, w_own, w_par, *after)


def attend(pos, lens, queries, d_context, keep, recv):
    wide = pl.BlockSpec((1, ATTEND, 512, 128), lambda m, p, n: (0, m, 0, 0))
    kv = pl.BlockSpec((ATTEND, 64, 256), lambda m, p, n: (m, 0, 0))
    return pl.pallas_call(
        attend_kernel,
        grid_spec=pltpu.PrefetchScalarGridSpec(
            num_scalar_prefetch=2,
            grid=(8 // ATTEND,),
            in_specs=[wide, wide, kv, kv],
            out_specs=[wide, wide, kv, kv],
        ),
        out_shape=[jax.ShapeDtypeStruct((1, 8, 512, 128), BF)] * 2
        + [jax.ShapeDtypeStruct((8, 64, 256), BF)] * 2,
        compiler_params=pltpu.CompilerParams(vmem_limit_bytes=12 * 2**20),
        name="attend",
    )(pos, lens, queries, d_context, keep, recv)


def total(parts):
    return functools.reduce(lambda p, q: p + q, [p.astype(F32) for p in parts]).astype(BF)


def shards(enc_final, enc_len, kv_weight, queries, d_context):
    section, mp = lax.axis_index("section"), lax.axis_index("mp")
    c = mp % 2
    pos = jnp.stack([section // 2, mp // 8, ((mp // 2) % 4) * 2 + section % 2, c]).astype(jnp.int32)
    first = c == 0

    local = enc_final[0]
    other = shift(local, dc=1)
    states = jnp.where(
        first, jnp.concatenate([local, other], 1), jnp.concatenate([other, local], 1)
    ).reshape(2, 64, 256)

    def halves(v, axis):
        lower, upper = lax.index_in_dim(v, 0, axis, False), lax.index_in_dim(v, 1, axis, False)
        return jnp.where(first, lower, upper), jnp.where(first, upper, lower)

    mine, _ = halves(states, 0)
    across = shift(mine, dz=4)
    got = []
    for k in (3, 2, 1):
        got.append(rise(states, k))
    near, passed = halves(jnp.stack(got), 1)
    passed = shift(passed, dc=1)
    line = jnp.concatenate([mine[None], near[::-1], across[None], passed], 0)

    w_own = kv_weight.reshape(16, 256, 256)
    w_par = shift(w_own, dc=1)

    slices = {0: line}
    for k in (1, 3, 2):
        slices[k] = cross(line, k, 1)
    low = jnp.stack([slices[0], slices[1]])
    high = jnp.stack([slices[2], slices[3]])
    right_low = cross(low, 1, 0)
    left_low = cross(low, 3, 0)
    left_high = cross(high, 3, 0)
    right_high = cross(high, 1, 0)
    far_low = cross(right_low, 1, 0)
    far_high = cross(left_high, 3, 0)
    near = (right_low, right_high, left_low, left_high)

    w_par, acc = project((0,), pos, (low, high), w_own, w_par, None, False)
    (acc,) = project((1, 3), pos, near, w_own, w_par, acc, False)
    keep, send = project((2,), pos, (far_low, far_high), w_own, w_par, acc, True)
    recv = shift(send, dc=1)
    context, query_grad, grad_keep, grad_send = attend(pos, enc_len, queries, d_context, keep, recv)
    grad_recv = shift(grad_send, dc=1)

    far_low_g, far_high_g = spread((2,), pos, grad_keep, grad_recv, w_own, w_par, ())
    pass_low = cross(far_low_g, 1, 0)
    pass_high = cross(far_high_g, 3, 0)
    right_low_g, right_high_g, left_low_g, left_high_g = spread(
        (1, 3), pos, grad_keep, grad_recv, w_own, w_par, (far_low_g,)
    )
    from_left_high = cross(right_high_g, 1, 0)
    from_right_low = cross(left_low_g, 3, 0)
    own_low, own_high = spread(
        (0,), pos, grad_keep, grad_recv, w_own, w_par, (right_low_g,)
    )
    from_left_low = cross(total([right_low_g, pass_low]), 1, 0)
    from_right_high = cross(total([left_high_g, pass_high]), 3, 0)

    states_in = (low, high, right_low, right_high, far_low, far_high, left_low, left_high)

    grad_own, grad_par = whole(
        weight_kernel, [VMEM] * 10, [((16, 256, 256), BF)] * 2, [VMEM] * 2, []
    )(pos, *states_in, grad_keep, grad_recv)
    grad_other = shift(grad_par, dc=1)
    weight_grad = total([grad_own, grad_other]).reshape(1, 4096, 2, 128)

    low = [total([own_low[k], from_left_low[k], from_right_low[k]]) for k in range(2)]
    high = [total([own_high[k], from_left_high[k], from_right_high[k]]) for k in range(2)]
    got = [low[0]]
    for k in (1, 3, 2):
        got.append(cross((low + high)[k], k, 1))
    passed = [total([p[8 - k] for p in got]) for k in (3, 2, 1)]
    passed = shift(jnp.stack(passed), dc=1)
    across = shift(total([p[4] for p in got]), dz=4)
    got_z = []
    for i, k in enumerate((3, 2, 1)):
        both = jnp.stack([total([p[k] for p in got]), passed[i]])
        got_z.append(rise(both, k).astype(F32))
    got_z[0], weight_grad = lax.optimization_barrier((got_z[0], weight_grad))
    both = got_z[0] + got_z[1] + got_z[2]
    mine = functools.reduce(lambda p, q: p + q, [p[0].astype(F32) for p in got])
    both = jnp.stack([both[0] + mine + across.astype(F32), both[1]]).reshape(2, 64, 2, 128)
    kept, passed = halves(both, 2)
    passed = shift(passed.astype(BF), dc=1).astype(F32)
    kept, far_half = (kept[0] + passed[1]).astype(BF), (kept[1] + passed[0]).astype(BF)
    enc_grad = jnp.where(
        first, jnp.concatenate([kept, far_half], 0), jnp.concatenate([far_half, kept], 0)
    )
    return context, query_grad, weight_grad, enc_grad[None]


def solution(mesh):
    return jax.shard_map(
        shards,
        mesh=mesh,
        in_specs=(
            P("section", None, "mp"),
            P(),
            P("section", None, None, "mp"),
            P("section", None, None, "mp"),
            P("section", None, None, "mp"),
        ),
        out_specs=(
            P("section", None, None, "mp"),
            P("section", None, None, "mp"),
            P("section", None, None, "mp"),
            P("section", None, "mp"),
        ),
        check_vma=False,
    )
```

```python
import functools
import math

import jax
import jax.numpy as jnp
from jax import lax
from jax.experimental import pallas as pl
from jax.experimental.pallas import tpu as pltpu
from jax.sharding import PartitionSpec as P

HD = 64
ATTEND = 2
AXES = ("section", "mp")
BF = jnp.bfloat16
F32 = jnp.float32


def coords(i):
    section, mp = divmod(i, 32)
    x, zl = divmod(section, 2)
    y, zh, c = mp // 8, (mp // 2) % 4, mp % 2
    return x, y, 2 * zh + zl, c


def index(x, y, z, c):
    return ((x % 4) * 2 + z % 2) * 32 + (y % 4) * 8 + ((z % 8) // 2) * 2 + c


def shift(value, dx=0, dy=0, dz=0, dc=0):
    pairs = []
    for i in range(256):
        x, y, z, c = coords(i)
        pairs.append((i, index(x + dx, y + dy, z + dz, c ^ dc)))
    return lax.ppermute(value, AXES, pairs)


def cross(value, k, along):
    pairs = []
    for i in range(256):
        x, y, z, c = coords(i)
        dx, dy = (k, 0) if c == along else (0, k)
        pairs.append((i, index(x + dx, y + dy, z, c)))
    return lax.ppermute(value, AXES, pairs)


def rise(value, k):
    pairs = []
    for i in range(256):
        x, y, z, c = coords(i)
        pairs.append((i, index(x, y, z - k if c else z + k, c)))
    return lax.ppermute(value, AXES, pairs)


def nt(a, b):
    return lax.dot_general(a, b, (((1,), (1,)), ((), ())), preferred_element_type=F32)


def nn(a, b):
    return lax.dot_general(a, b, (((1,), (0,)), ((), ())), preferred_element_type=F32)


def states_kernel(pos, local, other, states, mine):
    for core in range(2):

        @pl.when(pos[3] == core)
        def _():
            own, par = slice(core * 128, core * 128 + 128), slice(128 - core * 128, 256 - core * 128)
            for half in range(2):
                states[half, :, own] = local[half * 64 : half * 64 + 64]
                states[half, :, par] = other[half * 64 : half * 64 + 64]
            mine[:, own] = local[core * 64 : core * 64 + 64]
            mine[:, par] = other[core * 64 : core * 64 + 64]


def ends_kernel(pos, r3, r2, r1, p0, p1, p2, p3, across, kept, passed):
    both = r3[...].astype(F32) + r2[...].astype(F32) + r1[...].astype(F32)
    mine = across[...].astype(F32)
    for p in (p0, p1, p2, p3):
        mine += p[0].astype(F32)
    sums = (both[0] + mine, both[1])
    for core in range(2):

        @pl.when(pos[3] == core)
        def _():
            for half in range(2):
                kept[half] = sums[half][:, core * 128 : core * 128 + 128]
                passed[half] = sums[half][:, 128 - core * 128 : 256 - core * 128].astype(BF)


def result_kernel(pos, kept, passed, out):
    for half in range(2):
        total_half = (kept[half] + passed[1 - half].astype(F32)).astype(BF)
        for core in range(2):
            at = 64 * (half if core == 0 else 1 - half)

            @pl.when(pos[3] == core)
            def _():
                out[0, at : at + 64] = total_half


def slot_of(c, z, zh, zl):
    return ((1 - 2 * c) * (z - (2 * zh + zl)) + 16) & 7


def project_kernel(which, first, last, pos, *refs):
    n = len(which)
    x, y, z, c = pos[0], pos[1], pos[2], pos[3]
    pieces, (wo, wp), refs = refs[: 2 * n], refs[2 * n : 2 * n + 2], refs[2 * n + 2 :]
    if first:
        refs[0][...] = wp[...]
    else:
        before, refs = refs[0], refs[1:]
    acc = refs[-1]

    def product(dy, dxs, source):
        f = ((y + 4 - dy) & 3) * 4
        columns = []
        for zh in range(4):
            rows = [source(dx)[slot_of(c, z, zh, zl)] for dx in dxs for zl in range(2)]
            columns.append(jnp.concatenate(rows, axis=0))
        lhs = jnp.concatenate(columns, axis=1)
        own = nn(lhs, wo[pl.ds(f, 4)].reshape(1024, 256))
        return own, nn(lhs, wp[pl.ds(f, 4)].reshape(1024, 256))

    @pl.when(c == 0)
    def _():
        for dx in range(4):
            to = slice(dx * 128, dx * 128 + 128)
            if dx in which or first:
                acc[to] = jnp.zeros((128, 512), F32)
            else:
                acc[to] = before[to]
        for half in range(2):

            def step(inner, _):
                own, par = product(
                    2 * half + inner,
                    which,
                    lambda dx: pieces[2 * which.index(dx) + half].at[inner],
                )
                for i, dx in enumerate(which):
                    acc[dx * 128 : dx * 128 + 128, :256] += own[i * 128 : i * 128 + 128]
                    acc[dx * 128 : dx * 128 + 128, 256:] += par[i * 128 : i * 128 + 128]
                return 0

            lax.fori_loop(0, 2, step, 0)

    @pl.when(c == 1)
    def _():
        own, par = None, None
        for i, dy in enumerate(which):
            own_term, par_term = product(
                dy, range(4), lambda dx: pieces[2 * i + dx // 2].at[dx % 2]
            )
            own = own_term if own is None else own + own_term
            par = par_term if par is None else par + par_term
        if first:
            acc[:, :256] = own
            acc[:, 256:] = par
        else:
            acc[:, :256] = own + before[:, :256]
            acc[:, 256:] = par + before[:, 256:]

    if last:
        keep, send = refs[0], refs[1]
        for dx in range(4):
            for zl in range(2):
                m = ((x + 4 - dx) & 3) * 2 + zl
                row = (dx * 2 + zl) * 64
                keep[m] = acc[row : row + 64, :256].astype(BF)
                send[m] = acc[row : row + 64, 256:].astype(BF)


def attend_kernel(pos, lens, q_ref, d_ref, keep_ref, recv_ref, ctx_ref, qg_ref, own_ref, part_ref):
    left = lax.broadcasted_iota(jnp.int32, (128, 128), 1) < HD
    top = lax.broadcasted_iota(jnp.int32, (128, 128), 0) < HD
    zero = jnp.zeros((128, 128), BF)
    source = (lax.broadcasted_iota(jnp.int32, (128, 512), 0) + 64 * pos[3]) & 127
    factor = HD ** (-0.5)

    def stack_heads(t):
        return jnp.concatenate([jnp.where(left, t, zero), jnp.where(left, zero, t)], axis=0)

    def stack_heads_t(t):
        tt = t.T
        return jnp.concatenate([jnp.where(top, tt, zero), jnp.where(top, zero, tt)], axis=1)

    products = []
    for j in range(ATTEND):
        kv = jnp.concatenate([keep_ref[j], recv_ref[j]], axis=0)
        k, v = kv[:, :128], kv[:, 128:]
        products.append((k, v, nt(stack_heads(k), q_ref[0, j]), nt(stack_heads(v), d_ref[0, j])))
    for j, (k, v, scores, prob_grad) in enumerate(products):
        valid = source < lens[pl.program_id(0) * ATTEND + j]
        probs, score_grads = [], []
        for h in range(2):
            s = jnp.where(valid, scores[h * 128 : h * 128 + 128], -1e30)
            e = jnp.exp2((s - jnp.max(s, axis=0, keepdims=True)) * (factor * math.log2(math.e)))
            p = e * (1.0 / jnp.sum(e, axis=0, keepdims=True))
            g = prob_grad[h * 128 : h * 128 + 128]
            score_grads.append((p * (g - jnp.sum(g * p, axis=0, keepdims=True))).astype(BF))
            probs.append(p.astype(BF))
        prob = jnp.concatenate(probs, axis=0)
        score_grad = jnp.concatenate(score_grads, axis=0)
        ctx_ref[0, j] = nn(stack_heads_t(v), prob).astype(BF).T
        qg_ref[0, j] = nn(stack_heads_t(k * jnp.asarray(factor, BF)), score_grad).astype(BF).T
        vg = nn(prob, d_ref[0, j])
        kg = nn(score_grad, q_ref[0, j]) * factor
        kg = jnp.where(left, kg[:128], kg[128:]).astype(BF)
        vg = jnp.where(left, vg[:128], vg[128:]).astype(BF)
        own_ref[j, :, :128] = kg[:64]
        own_ref[j, :, 128:] = vg[:64]
        part_ref[j, :, :128] = kg[64:]
        part_ref[j, :, 128:] = vg[64:]


def spread_kernel(which, after, pos, g_own, g_par, wo, wp, *refs):
    outs = refs[after:]
    x, y, z, c = pos[0], pos[1], pos[2], pos[3]

    def product(dxs):
        order = [((x + dx) & 3) * 2 + zl for dx in dxs for zl in range(2)]
        own = jnp.concatenate([g_own[m] for m in order], axis=0)
        par = jnp.concatenate([g_par[m] for m in order], axis=0)

        def emit(dy, target):
            yy = (y + dy) & 3
            t = nt(own, wo[pl.ds(yy * 4, 4)].reshape(1024, 256))
            t = (t + nt(par, wp[pl.ds(yy * 4, 4)].reshape(1024, 256))).astype(BF)
            for i, dx in enumerate(dxs):
                for zl in range(2):
                    row = i * 128 + zl * 64
                    for zh in range(4):
                        target(dx)[slot_of(1 - c, z, zh, zl)] = t[
                            row : row + 64, zh * 256 : zh * 256 + 256
                        ]

        return emit

    @pl.when(c == 0)
    def _():
        emit = product(which)
        for half in range(2):

            def step(inner, _):
                emit(2 * half + inner, lambda dx: outs[2 * which.index(dx) + half].at[inner])
                return 0

            lax.fori_loop(0, 2, step, 0)

    @pl.when(c == 1)
    def _():
        emit = product(range(4))
        for i, dy in enumerate(which):
            emit(dy, lambda dx: outs[2 * i + dx // 2].at[dx % 2])


def weight_kernel(pos, *refs):
    pieces, (g_own, g_par, _, own_ref, par_ref) = refs[:8], refs[8:]
    x, y, z, c = pos[0], pos[1], pos[2], pos[3]
    order = [((x + 4 - dx) & 3) * 2 + zl for dx in range(4) for zl in range(2)]
    own = jnp.concatenate([g_own[m] for m in order], axis=0)
    par = jnp.concatenate([g_par[m] for m in order], axis=0)
    grads = jnp.concatenate([own, par], axis=1).T

    def emit(dy, zh, source):
        rows = [source(dx)[slot_of(c, z, zh, zl)] for dx in range(4) for zl in range(2)]
        out = nn(grads, jnp.concatenate(rows, axis=0)).astype(BF).T
        f = ((y + 4 - dy) & 3) * 4 + zh
        own_ref[f] = out[:, :256]
        par_ref[f] = out[:, 256:]

    @pl.when(c == 0)
    def _():
        for half in range(2):

            def step(i, _):
                inner = i // 4
                emit(2 * half + inner, i & 3, lambda dx: pieces[2 * dx + half].at[inner])
                return 0

            lax.fori_loop(0, 8, step, 0)

    @pl.when(c == 1)
    def _():
        for dy in range(4):

            def step(zh, _):
                emit(dy, zh, lambda dx: pieces[2 * dy + dx // 2].at[dx % 2])
                return 0

            lax.fori_loop(0, 4, step, 0)


SMEM = pl.BlockSpec(memory_space=pltpu.SMEM)
VMEM = pl.BlockSpec(memory_space=pltpu.VMEM)
HBM = pl.BlockSpec(memory_space=pl.ANY)


def whole(kernel, ins, outs, out_specs, scratch):
    return pl.pallas_call(
        kernel,
        in_specs=[SMEM] + ins,
        out_specs=out_specs,
        out_shape=[jax.ShapeDtypeStruct(s, d) for s, d in outs],
        scratch_shapes=scratch,
        compiler_params=pltpu.CompilerParams(vmem_limit_bytes=12 * 2**20),
    )


def project(which, pos, pieces, w_own, w_par, before, last):
    first = before is None
    acc = ((512, 512), F32)
    half = ((8, 64, 256), BF)
    outs = [half, half] if last else [acc]
    if first:
        outs = [((16, 256, 256), BF), acc]
    return whole(
        functools.partial(project_kernel, which, first, last),
        [VMEM] * (2 * len(which) + (2 if first else 3)),
        outs,
        [VMEM] * len(outs),
        [pltpu.VMEM((512, 512), F32)] if last else [],
    )(pos, *pieces, w_own, w_par, *([] if first else [before]))


def spread(which, pos, own, par, w_own, w_par, after):
    return whole(
        functools.partial(spread_kernel, which, len(after)),
        [VMEM] * 4 + [HBM] * len(after),
        [((2, 8, 64, 256), BF)] * (2 * len(which)),
        [VMEM] * (2 * len(which)),
        [],
    )(pos, own, par, w_own, w_par, *after)


def attend(pos, lens, queries, d_context, keep, recv):
    wide = pl.BlockSpec((1, ATTEND, 512, 128), lambda m, p, n: (0, m, 0, 0))
    kv = pl.BlockSpec((ATTEND, 64, 256), lambda m, p, n: (m, 0, 0))
    return pl.pallas_call(
        attend_kernel,
        grid_spec=pltpu.PrefetchScalarGridSpec(
            num_scalar_prefetch=2,
            grid=(8 // ATTEND,),
            in_specs=[wide, wide, kv, kv],
            out_specs=[wide, wide, kv, kv],
        ),
        out_shape=[jax.ShapeDtypeStruct((1, 8, 512, 128), BF)] * 2
        + [jax.ShapeDtypeStruct((8, 64, 256), BF)] * 2,
        compiler_params=pltpu.CompilerParams(vmem_limit_bytes=12 * 2**20),
        name="attend",
    )(pos, lens, queries, d_context, keep, recv)


def total(parts):
    return functools.reduce(lambda p, q: p + q, [p.astype(F32) for p in parts]).astype(BF)


def shards(enc_final, enc_len, kv_weight, queries, d_context):
    section, mp = lax.axis_index("section"), lax.axis_index("mp")
    c = mp % 2
    pos = jnp.stack([section // 2, mp // 8, ((mp // 2) % 4) * 2 + section % 2, c]).astype(jnp.int32)
    first = c == 0

    local = enc_final[0]
    other = shift(local, dc=1)
    states, mine = whole(
        states_kernel, [VMEM] * 2, [((2, 64, 256), BF), ((64, 256), BF)], [VMEM] * 2, []
    )(pos, local, other)

    def halves(v, axis):
        lower, upper = lax.index_in_dim(v, 0, axis, False), lax.index_in_dim(v, 1, axis, False)
        return jnp.where(first, lower, upper), jnp.where(first, upper, lower)

    across = shift(mine, dz=4)
    got = []
    for k in (3, 2, 1):
        got.append(rise(states, k))
    near, passed = halves(jnp.stack(got), 1)
    passed = shift(passed, dc=1)
    line = jnp.concatenate([mine[None], near[::-1], across[None], passed], 0)

    w_own = kv_weight.reshape(16, 256, 256)
    w_par = shift(w_own, dc=1)

    slices = {0: line}
    for k in (1, 3, 2):
        slices[k] = cross(line, k, 1)
    low = jnp.stack([slices[0], slices[1]])
    high = jnp.stack([slices[2], slices[3]])
    right_low = cross(low, 1, 0)
    left_low = cross(low, 3, 0)
    left_high = cross(high, 3, 0)
    right_high = cross(high, 1, 0)
    far_low = cross(right_low, 1, 0)
    far_high = cross(left_high, 3, 0)
    near = (right_low, right_high, left_low, left_high)

    w_par, acc = project((0,), pos, (low, high), w_own, w_par, None, False)
    (acc,) = project((1, 3), pos, near, w_own, w_par, acc, False)
    keep, send = project((2,), pos, (far_low, far_high), w_own, w_par, acc, True)
    recv = shift(send, dc=1)
    context, query_grad, grad_keep, grad_send = attend(pos, enc_len, queries, d_context, keep, recv)
    grad_recv = shift(grad_send, dc=1)

    far_low_g, far_high_g = spread((2,), pos, grad_keep, grad_recv, w_own, w_par, ())
    pass_low = cross(far_low_g, 1, 0)
    pass_high = cross(far_high_g, 3, 0)
    right_low_g, right_high_g, left_low_g, left_high_g = spread(
        (1, 3), pos, grad_keep, grad_recv, w_own, w_par, (far_low_g,)
    )
    from_left_high = cross(right_high_g, 1, 0)
    from_right_low = cross(left_low_g, 3, 0)
    own_low, own_high = spread(
        (0,), pos, grad_keep, grad_recv, w_own, w_par, (right_low_g,)
    )
    from_left_low = cross(total([right_low_g, pass_low]), 1, 0)
    from_right_high = cross(total([left_high_g, pass_high]), 3, 0)

    grad_own, grad_par = whole(
        weight_kernel, [VMEM] * 10 + [HBM], [((16, 256, 256), BF)] * 2, [VMEM] * 2, []
    )(pos, low, high, right_low, right_high, far_low, far_high, left_low, left_high, grad_keep, grad_recv, own_low)
    grad_other = shift(grad_par, dc=1)
    weight_grad = total([grad_own, grad_other]).reshape(1, 4096, 2, 128)

    low = [total([own_low[k], from_left_low[k], from_right_low[k]]) for k in range(2)]
    high = [total([own_high[k], from_left_high[k], from_right_high[k]]) for k in range(2)]
    got = [low[0]]
    for k in (1, 3, 2):
        got.append(cross((low + high)[k], k, 1))
    passed = [total([p[8 - k] for p in got]) for k in (3, 2, 1)]
    passed = shift(jnp.stack(passed), dc=1)
    across = shift(total([p[4] for p in got]), dz=4)
    got_z = []
    for i, k in enumerate((3, 2, 1)):
        both = jnp.stack([total([p[k] for p in got]), passed[i]])
        got_z.append(rise(both, k))
    got_z[0], weight_grad = lax.optimization_barrier((got_z[0], weight_grad))
    kept, passed = whole(
        ends_kernel, [VMEM] * 8, [((2, 64, 128), F32), ((2, 64, 128), BF)], [VMEM] * 2, []
    )(pos, *got_z, *got, across)
    passed = shift(passed, dc=1)
    (enc_grad,) = whole(
        result_kernel, [VMEM] * 2, [((1, 128, 128), BF)], [VMEM], []
    )(pos, kept, passed)
    return context, query_grad, weight_grad, enc_grad


def solution(mesh):
    return jax.shard_map(
        shards,
        mesh=mesh,
        in_specs=(
            P("section", None, "mp"),
            P(),
            P("section", None, None, "mp"),
            P("section", None, None, "mp"),
            P("section", None, None, "mp"),
        ),
        out_specs=(
            P("section", None, None, "mp"),
            P("section", None, None, "mp"),
            P("section", None, None, "mp"),
            P("section", None, "mp"),
        ),
        check_vma=False,
    )
```
